32 devices in a mesh: dp: 16 (over z, x, core), tp: 2 (over y).
Axes of the slice: x: 2, y: 2, z: 4, core: 2. Of those that a mesh axis runs over, the one named last changes fastest.
Arguments:
- tokens: bfloat16 [3072, 3584], P('dp', 'tp'), may hold values from -6 to 6
- cotangent: bfloat16 [3072, 3584], P('dp', 'tp'), may hold values from -6 to 6
- working: bfloat16 [16, 2, 3, 2048, 3584], P('dp', 'tp'), may hold values from -0.09375 to 0.09375
- degraded: int32 [16], P('dp'), may hold values from 0 to 1, as said below
- block_map: int32 [16, 16], P('dp'), may hold values from 0 to 1, as said below
- master: float32 [3, 2048, 3584], P(None, ('tp', 'dp')), may hold values from -6 to 6
- moment_one: float32 [3, 2048, 3584], P(None, ('tp', 'dp')), may hold values from -6 to 6
- moment_two: float32 [3, 2048, 3584], P(None, ('tp', 'dp')), may hold values from 0.5 to 8
Outputs:
- input_grad: bfloat16 [3072, 3584], P('dp', 'tp')
- master_next: float32 [3, 2048, 3584], P(None, ('tp', 'dp'))
- moment_one_next: float32 [3, 2048, 3584], P(None, ('tp', 'dp'))
- moment_two_next: float32 [3, 2048, 3584], P(None, ('tp', 'dp'))
The draws below stay inside these ranges and needn't reach their ends.
Inputs may be any that keep to these rules, and one draw needn't show every extreme that they name: `degraded`: exactly 4 replicas have the value 1. `block_map`: in every row the 16 blocks lie on 1 distinct devices, each of which holds 16 or 16 of them, and at least one holds 16. A row is read only where degraded is 1.
All inputs are finite; a program needn't handle non-finite values.
Results may differ from the reference program's by a relative error of at most 0.0075.
Values may be sent and summed in bfloat16 or wider, within the bound.
No kernel may reach another device: no remote copies, remote signals or barrier semaphores. Data moves between devices by JAX's collectives and lax.ppermute only.
A program may use at most 128 MiB of HBM per device.

```python
import math
import jax
import jax.numpy as jnp
from jax import lax

D = 3584
BLOCK = 128
BLOCKS = 16
FF = 2048
TOK = 192
TOKENS = 3072
USED = 1
SLOTS = 16
N_DP = 16
N_TP = 2


def draw_degraded(key, part):
    shuffled = jax.random.permutation(key, N_DP).astype(jnp.int32)
    return (shuffled < N_DP // 4).astype(jnp.int32)


def draw_block_map(key, part):

    def one_row(row_index):
        row_key = jax.random.fold_in(key, row_index)
        devices = jax.random.permutation(jax.random.fold_in(row_key, 1), N_TP).astype(jnp.int32)
        block_order = jax.random.permutation(jax.random.fold_in(row_key, 2), BLOCKS).astype(jnp.int32)
        holder = devices[jnp.arange(BLOCKS, dtype=jnp.int32) % USED]
        return jnp.zeros((BLOCKS,), jnp.int32).at[block_order].set(holder)
    return jax.vmap(one_row)(jnp.arange(N_DP, dtype=jnp.int32))


def levels(key, extent, shards, least, high):
    def one(axis_at, blocks):
        heights = jax.random.uniform(jax.random.fold_in(jax.random.fold_in(key, 6), axis_at), (blocks,), jnp.float32, least / len(shards), high / len(shards))
        return jnp.repeat(jnp.exp(heights), extent[axis_at] // blocks).reshape((-1,) + (1,) * (len(extent) - axis_at - 1))

    level = one(*shards[0])
    for cut in shards[1:]:
        level = level * one(*cut)
    return level


def scatter_about(rng, shape, scale, reach, shards=(), kind=jnp.bfloat16):
    entries = scale * jax.random.normal(rng, shape, jnp.float32)
    if shards:
        entries = entries * levels(rng, shape, shards, -0.22, 0.18)
    return jnp.clip(entries, -reach, reach).astype(kind)


def setup_inputs(seed: int = 0) -> dict:
    splits = jax.random.split(jax.random.key(seed), 9)
    tokens = scatter_about(splits[0], (TOKENS, D), 1.0, 6.0, ((0, 16), (1, 2)))
    cotangent = scatter_about(splits[1], (TOKENS, D), 1.0, 6.0, ((0, 16), (1, 2)))
    working = scatter_about(splits[2], (N_DP, N_TP, 3, SLOTS * BLOCK, D), D ** -0.5, 0.09375, ((0, 16), (1, 2)))
    degraded = draw_degraded(jax.random.fold_in(splits[8], 71), 0)
    block_map = draw_block_map(jax.random.fold_in(splits[8], 71), 0)
    master = scatter_about(splits[5], (3, FF, D), 1.0, 6.0, ((1, 32),), jnp.float32)
    moment_one = scatter_about(splits[6], (3, FF, D), 1.0, 6.0, ((1, 32),), jnp.float32)
    moment_two = jnp.clip(jnp.exp(math.log(8.0) - 2.7725887 * jax.random.uniform(splits[7], (3, FF, D), jnp.float32) ** levels(splits[7], (3, FF, D), ((1, 32),), -0.2, 0.2)), 0.5, 8.0)
    return dict(tokens=tokens, cotangent=cotangent, working=working, degraded=degraded, block_map=block_map, master=master, moment_one=moment_one, moment_two=moment_two)


beta_one = 0.9
beta_two = 0.95
learn_rate = 0.05
decay_rate = 0.1
adam_eps = 1e-08
bias_one = 1.0 - 0.9 ** 10
bias_two = 1.0 - 0.95 ** 10

def layout_places(replica_flag, mapping):
    blocks = jnp.arange(BLOCKS, dtype=jnp.int32)
    canonical = (blocks // (BLOCKS // N_TP)).astype(jnp.int32)
    holder = jnp.where(replica_flag > 0, mapping, canonical).astype(jnp.int32)
    earlier = (holder[None, :] == holder[:, None]) & (blocks[None, :] < blocks[:, None])
    slot_rank = lax.optimization_barrier(jnp.sum(earlier.astype(jnp.int32), axis=1)).astype(jnp.int32)
    return (holder * SLOTS + slot_rank).astype(jnp.int32)

def replica_step(running, items):
    tok_rep, cot_rep, work_rep, replica_flag, mapping = items
    places = layout_places(replica_flag, mapping)
    stacked = work_rep.reshape(N_TP, 3, SLOTS, BLOCK, D).transpose(0, 2, 1, 3, 4).reshape(N_TP * SLOTS, 3, BLOCK, D)
    chosen = jnp.take(stacked, places, axis=0)
    weights = chosen.transpose(1, 0, 2, 3).reshape(3, FF, D)
    contract_d = (((1,), (1,)), ((), ()))
    gate_pre = lax.dot_general(tok_rep, weights[0], contract_d, preferred_element_type=jnp.float32)
    up_pre = lax.dot_general(tok_rep, weights[1], contract_d, preferred_element_type=jnp.float32)
    hidden_grad = lax.dot_general(cot_rep, weights[2], contract_d, preferred_element_type=jnp.float32)
    gate_sig = jax.nn.sigmoid(gate_pre)
    active = gate_pre * gate_sig
    hidden = (active * up_pre).astype(jnp.bfloat16)
    gate_grad = (hidden_grad * up_pre * gate_sig * (1.0 + gate_pre * (1.0 - gate_sig))).astype(jnp.bfloat16)
    up_grad = (hidden_grad * active).astype(jnp.bfloat16)
    input_rep = (jnp.dot(gate_grad, weights[0], preferred_element_type=jnp.float32) + jnp.dot(up_grad, weights[1], preferred_element_type=jnp.float32)).astype(jnp.bfloat16)
    contract_t = (((0,), (0,)), ((), ()))
    gate_term = lax.dot_general(gate_grad, tok_rep, contract_t, preferred_element_type=jnp.float32)
    up_term = lax.dot_general(up_grad, tok_rep, contract_t, preferred_element_type=jnp.float32)
    down_term = lax.dot_general(hidden, cot_rep, contract_t, preferred_element_type=jnp.float32)
    return (running + jnp.stack([gate_term, up_term, down_term], axis=0), input_rep)

def reference(tokens, cotangent, working, degraded, block_map, master, moment_one, moment_two):
    items = (tokens.reshape(N_DP, TOK, D), cotangent.reshape(N_DP, TOK, D), working, degraded, block_map)
    initial = jnp.zeros((3, FF, D), jnp.float32)
    summed, inputs_all = lax.scan(replica_step, initial, items)
    grad_mean = summed / N_DP
    moment_one_next = beta_one * moment_one + (1.0 - beta_one) * grad_mean
    moment_two_next = beta_two * moment_two + (1.0 - beta_two) * grad_mean * grad_mean
    update = moment_one_next / bias_one / (jnp.sqrt(moment_two_next / bias_two) + adam_eps) + decay_rate * master
    master_next = master - learn_rate * update
    return (inputs_all.reshape(TOKENS, D), master_next, moment_one_next, moment_two_next)
```

```python
import jax
import jax.numpy as jnp
from jax import lax
from jax.experimental import pallas as pl
from jax.experimental.pallas import tpu as pltpu
from jax.sharding import PartitionSpec as P

BLOCK = 128
BLOCKS = 16


beta_one = 0.9
beta_two = 0.95
learn_rate = 0.05
decay_rate = 0.1
adam_eps = 1e-08
bias_one = 1.0 - 0.9**10
bias_two = 1.0 - 0.95**10


def layout_places(replica_flag, mapping, tp_size, slot_count):
    blocks = jnp.arange(BLOCKS, dtype=jnp.int32)
    canonical = blocks // (BLOCKS // tp_size)
    holder = jnp.where(replica_flag > 0, mapping, canonical)
    earlier = (holder[None, :] == holder[:, None]) & (blocks[None, :] < blocks[:, None])
    slot_rank = jnp.sum(earlier.astype(jnp.int32), axis=1)
    return holder * slot_count + slot_rank


def per_device(tokens, cotangent, working, degraded, block_map, master, moment_one, moment_two):
    tp_size = lax.axis_size("tp")
    replicas = lax.axis_size("dp")
    my_index = lax.axis_index("tp")
    weights = working[0, 0]
    slot_count = weights.shape[1] // BLOCK
    per_dev = BLOCKS // tp_size
    places = layout_places(degraded[0], block_map[0], tp_size, slot_count)
    my_slots = my_index * slot_count + jnp.arange(slot_count, dtype=jnp.int32)
    holding = places[:, None] == my_slots[None, :]
    filled = jnp.any(holding, axis=0).astype(jnp.float32)
    column_mask = jnp.repeat(filled, BLOCK)
    inputs, upstream = (
        lax.all_gather(tokens, "tp", axis=1, tiled=True),
        lax.all_gather(cotangent, "tp", axis=1, tiled=True),
    )
    contract_d = (((1,), (1,)), ((), ()))
    gate_pre = lax.dot_general(inputs, weights[0], contract_d, preferred_element_type=jnp.float32)
    up_pre = lax.dot_general(inputs, weights[1], contract_d, preferred_element_type=jnp.float32)
    hidden_grad = lax.dot_general(
        upstream, weights[2], contract_d, preferred_element_type=jnp.float32
    )
    gate_sig = jax.nn.sigmoid(gate_pre)
    active = gate_pre * gate_sig
    hidden = (active * up_pre * column_mask).astype(jnp.bfloat16)
    gate_grad = (
        hidden_grad * up_pre * gate_sig * (1.0 + gate_pre * (1.0 - gate_sig)) * column_mask
    ).astype(jnp.bfloat16)
    up_grad = (hidden_grad * active * column_mask).astype(jnp.bfloat16)
    partial_value = jnp.dot(gate_grad, weights[0], preferred_element_type=jnp.float32) + jnp.dot(
        up_grad, weights[1], preferred_element_type=jnp.float32
    )
    input_grad = lax.psum_scatter(partial_value, "tp", scatter_dimension=1, tiled=True).astype(
        jnp.bfloat16
    )
    tok_rows = gate_grad.shape[0]
    packed = jnp.stack(
        [
            hidden.reshape(tok_rows, slot_count, BLOCK),
            gate_grad.reshape(tok_rows, slot_count, BLOCK),
            up_grad.reshape(tok_rows, slot_count, BLOCK),
        ],
        axis=2,
    )
    packed = packed.transpose(1, 0, 2, 3).reshape(slot_count, tok_rows, 3 * BLOCK)
    selector = holding.astype(jnp.bfloat16)
    outgoing = jnp.einsum(
        "qs,stc->qtc", selector, packed, preferred_element_type=jnp.float32
    ).astype(jnp.bfloat16)
    incoming = lax.all_to_all(outgoing, "tp", split_axis=0, concat_axis=0, tiled=True)
    owned_acts = jnp.sum(incoming.reshape(tp_size, per_dev, tok_rows, 3 * BLOCK), axis=0)
    owned_kinds = (
        owned_acts.reshape(per_dev, tok_rows, 3, BLOCK)
        .transpose(2, 1, 0, 3)
        .reshape(3, tok_rows, per_dev * BLOCK)
    )
    contract_t = (((0,), (0,)), ((), ()))
    gate_term = lax.dot_general(
        owned_kinds[1], inputs, contract_t, preferred_element_type=jnp.float32
    )
    up_term = lax.dot_general(
        owned_kinds[2], inputs, contract_t, preferred_element_type=jnp.float32
    )
    down_term = lax.dot_general(
        owned_kinds[0], upstream, contract_t, preferred_element_type=jnp.float32
    )
    summed = lax.psum_scatter(
        jnp.stack([gate_term, up_term, down_term], axis=1).astype(jnp.bfloat16),
        "dp",
        scatter_dimension=0,
        tiled=True,
    ).astype(jnp.float32)
    grad_mean = jnp.transpose(summed, (1, 0, 2)) / replicas
    moment_one_next = beta_one * moment_one + (1.0 - beta_one) * grad_mean
    moment_two_next = beta_two * moment_two + (1.0 - beta_two) * grad_mean * grad_mean
    update = (
        moment_one_next / bias_one / (jnp.sqrt(moment_two_next / bias_two) + adam_eps)
        + decay_rate * master
    )
    master_next = master - learn_rate * update
    return (input_grad, master_next, moment_one_next, moment_two_next)


CORES = 2
PAIR = 2
contract_last = (((1,), (1,)), ((), ()))
contract_mid = (((1,), (0,)), ((), ()))
contract_first = (((0,), (0,)), ((), ()))


def dot32(a, b, dims):
    return lax.dot_general(a, b, dims, preferred_element_type=jnp.float32)


def weight_specs(kinds, half, sides):
    specs = []
    for kind in kinds:
        for side in sides:
            for j in range(PAIR):

                def where(i, s, kind=kind, side=side, j=j):
                    column = s[2 * s.shape[0] // 3] if side == 0 else 1 - s[2 * s.shape[0] // 3]
                    return (0, 0, kind, s[PAIR * i + j], column)

                specs.append(pl.BlockSpec((1, 1, 1, BLOCK, half), where))
    return specs


def whole_spec(shape):
    return pl.BlockSpec(shape, lambda *_: (0,) * len(shape))


def both(first, second):
    return jnp.concatenate([first[0, 0, 0], second[0, 0, 0]], axis=0)


def gate_up(scalars, own, other, working):
    pairs = scalars.shape[0] // 6
    rows, half = own.shape

    def body(s, own_ref, other_ref, *refs):
        weights, (gate_ref, up_ref) = refs[:8], refs[8:]
        i = pl.program_id(0)
        held = s[2 * pairs + 2 * i] + s[2 * pairs + 2 * i + 1]

        @pl.when(held > 0)
        def _():
            for at, ref in ((0, gate_ref), (4, up_ref)):
                ref[0] = dot32(own_ref[...], both(*weights[at : at + 2]), contract_last) + dot32(
                    other_ref[...], both(*weights[at + 2 : at + 4]), contract_last
                )

    out = jax.ShapeDtypeStruct((pairs, rows, PAIR * BLOCK), jnp.float32)
    out_spec = pl.BlockSpec((1, rows, PAIR * BLOCK), lambda i, s: (i, 0, 0))
    return pl.pallas_call(
        body,
        out_shape=(out, out),
        grid_spec=pltpu.PrefetchScalarGridSpec(
            num_scalar_prefetch=1,
            grid=(pairs,),
            in_specs=[whole_spec(own.shape)] * 2 + weight_specs((0, 1), half, (0, 1)),
            out_specs=(out_spec, out_spec),
        ),
        cost_estimate=pl.CostEstimate(
            flops=8 * rows * half * pairs * PAIR * BLOCK,
            bytes_accessed=8 * half * pairs * PAIR * BLOCK,
            transcendentals=0,
        ),
        name="gate_up",
    )(scalars, own, other, *[working] * 8)


def down_acts(scalars, own, other, working, gate, up):
    pairs = scalars.shape[0] // 6
    quarter = pairs // 4
    rows, half = own.shape
    narrow = BLOCK // CORES

    def body(s, own_ref, other_ref, w0, w1, w2, w3, gate_ref, up_ref, theirs, far, near, grads):
        i = pl.program_id(0)
        has = [s[2 * pairs + 2 * i + j] for j in range(PAIR)]
        core = s[4 * pairs + 1]
        targets = ((i < 2 * quarter, theirs), ((i >= 2 * quarter) & (i < 3 * quarter), far), (i >= 3 * quarter, near))

        def put(values):
            for at, (mine, ref) in enumerate(targets):

                @pl.when(mine)
                def _(ref=ref, at=at):
                    for kind, value in enumerate(values):
                        for c in range(CORES):
                            piece = jnp.concatenate(
                                [
                                    value[:, j * BLOCK + c * narrow : j * BLOCK + (c + 1) * narrow]
                                    for j in range(PAIR)
                                ],
                                axis=1,
                            ).astype(jnp.bfloat16)
                            slot = jnp.bitwise_xor(core, c)
                            if at == 0:
                                ref[0, slot, 0, kind] = piece
                            else:
                                ref[slot, 0, kind] = piece

        @pl.when(has[0] + has[1] > 0)
        def _():
            dh = dot32(own_ref[...], both(w0, w1), contract_last) + dot32(
                other_ref[...], both(w2, w3), contract_last
            )
            lane = lax.broadcasted_iota(jnp.int32, dh.shape, 1)
            keep = jnp.where(lane < BLOCK, has[0], has[1]) > 0
            zg, zu = gate_ref[0], up_ref[0]
            sig = jax.nn.sigmoid(zg)
            act = zg * sig
            hidden = jnp.where(keep, act * zu, 0.0)
            dgate = jnp.where(keep, dh * zu * sig * (1.0 + zg * (1.0 - sig)), 0.0)
            dup = jnp.where(keep, dh * act, 0.0)
            grads[0, 0] = dgate.astype(jnp.bfloat16)
            grads[0, 1] = dup.astype(jnp.bfloat16)
            put((dgate, dup, hidden))

        @pl.when(has[0] + has[1] == 0)
        def _():
            zero = jnp.zeros((rows, PAIR * BLOCK), jnp.float32)
            grads[...] = jnp.zeros(grads.shape, grads.dtype)
            put((zero, zero, zero))

    part = (quarter, 3, rows, BLOCK)
    z_spec = pl.BlockSpec((1, rows, PAIR * BLOCK), lambda i, s: (i, 0, 0))

    def theirs_at(i, s):
        at = jnp.minimum(i, 2 * quarter - 1)
        return (at // quarter, 0, at % quarter, 0, 0, 0)

    return pl.pallas_call(
        body,
        out_shape=(
            jax.ShapeDtypeStruct((2, CORES, *part), jnp.bfloat16),
            jax.ShapeDtypeStruct((CORES, *part), jnp.bfloat16),
            jax.ShapeDtypeStruct((CORES, *part), jnp.bfloat16),
            jax.ShapeDtypeStruct((pairs, 2, rows, PAIR * BLOCK), jnp.bfloat16),
        ),
        grid_spec=pltpu.PrefetchScalarGridSpec(
            num_scalar_prefetch=1,
            grid=(pairs,),
            in_specs=[whole_spec(own.shape)] * 2 + weight_specs((2,), half, (0, 1)) + [z_spec, z_spec],
            out_specs=(
                pl.BlockSpec((1, CORES, 1, 3, rows, BLOCK), theirs_at),
                pl.BlockSpec(
                    (CORES, 1, 3, rows, BLOCK),
                    lambda i, s: (0, jnp.clip(i - 2 * quarter, 0, quarter - 1), 0, 0, 0),
                ),
                pl.BlockSpec(
                    (CORES, 1, 3, rows, BLOCK),
                    lambda i, s: (0, jnp.clip(i - 3 * quarter, 0, quarter - 1), 0, 0, 0),
                ),
                pl.BlockSpec((1, 2, rows, PAIR * BLOCK), lambda i, s: (i, 0, 0, 0)),
            ),
        ),
        cost_estimate=pl.CostEstimate(
            flops=4 * rows * half * pairs * PAIR * BLOCK,
            bytes_accessed=4 * half * pairs * PAIR * BLOCK + 12 * rows * pairs * PAIR * BLOCK,
            transcendentals=rows * pairs * PAIR * BLOCK,
        ),
        name="down_acts",
    )(scalars, own, other, *[working] * 4, gate, up)


def input_part(scalars, grads, working, half, side):
    pairs = scalars.shape[0] // 6
    rows = grads.shape[2]

    def body(s, grads_ref, w0, w1, w2, w3, out_ref, total):
        i = pl.program_id(0)

        @pl.when(i == 0)
        def _():
            total[...] = jnp.zeros(total.shape, total.dtype)

        @pl.when(s[2 * pairs + 2 * i] + s[2 * pairs + 2 * i + 1] > 0)
        def _():
            total[...] += dot32(grads_ref[0, 0], both(w0, w1), contract_mid) + dot32(
                grads_ref[0, 1], both(w2, w3), contract_mid
            )

        @pl.when(i == pairs - 1)
        def _():
            out_ref[...] = total[...].astype(out_ref.dtype)

    return pl.pallas_call(
        body,
        out_shape=jax.ShapeDtypeStruct((rows, half), jnp.bfloat16 if side else jnp.float32),
        grid_spec=pltpu.PrefetchScalarGridSpec(
            num_scalar_prefetch=1,
            grid=(pairs,),
            in_specs=[pl.BlockSpec((1, 2, rows, PAIR * BLOCK), lambda i, s: (i, 0, 0, 0))]
            + weight_specs((0, 1), half, (side,)),
            out_specs=whole_spec((rows, half)),
            scratch_shapes=[pltpu.VMEM((rows, half), jnp.float32)],
        ),
        cost_estimate=pl.CostEstimate(
            flops=4 * rows * half * pairs * PAIR * BLOCK,
            bytes_accessed=4 * half * pairs * PAIR * BLOCK,
            transcendentals=0,
        ),
        name="input_other" if side else "input_own",
    )(scalars, grads, *[working] * 4)


def weight_grad(acts, tokens, cotangents, replicas):
    group = len(acts)
    quarter, _, rows, _ = acts[0].shape[-4:]
    half = tokens[0].shape[1]
    narrow = BLOCK // CORES
    wide = quarter * BLOCK
    tile = 256 if half % 256 == 0 else BLOCK

    def body(*refs):
        a_refs, t_refs, c_refs = refs[:group], refs[group : 2 * group], refs[2 * group : 3 * group]
        out_ref, left = refs[3 * group :]

        @pl.when(pl.program_id(0) == 0)
        def _():
            for r, ref in enumerate(a_refs):
                value = ref[0] if len(ref.shape) == 5 else ref
                for kind in range(3):
                    for p in range(quarter):
                        block = value[p, kind] if len(ref.shape) == 5 else ref[p, kind]
                        left[kind, r, :, p * BLOCK : (p + 1) * BLOCK] = block

        for kind in range(3):
            lhs = jnp.concatenate([left[kind, r] for r in range(group)], axis=0)
            rhs = jnp.concatenate([ref[...] for ref in (c_refs if kind == 2 else t_refs)], axis=0)
            value = dot32(lhs, rhs, contract_first).astype(jnp.bfloat16)
            for z in range(2 * quarter):
                out_ref[z, kind] = value[z * narrow : (z + 1) * narrow]

    def act_spec(a):
        if a.ndim == 5:
            return pl.BlockSpec((1, *a.shape[1:]), lambda i: (0,) * 5)
        return pl.BlockSpec(a.shape, lambda i: (0,) * 4)

    x_spec = pl.BlockSpec((rows, tile), lambda i: (0, i))
    return pl.pallas_call(
        body,
        out_shape=jax.ShapeDtypeStruct((2 * quarter, 3, narrow, half), jnp.bfloat16),
        grid=(half // tile,),
        in_specs=[act_spec(a) for a in acts] + [x_spec] * (2 * group),
        out_specs=pl.BlockSpec((2 * quarter, 3, narrow, tile), lambda i: (0, 0, 0, i)),
        scratch_shapes=[pltpu.VMEM((3, group, rows, wide), jnp.bfloat16)],
        cost_estimate=pl.CostEstimate(
            flops=6 * group * rows * wide * half,
            bytes_accessed=4 * group * rows * half + 6 * wide * half,
            transcendentals=0,
        ),
        name="weight_grad",
    )(*acts, *tokens, *cotangents)


def adam(place, arrived, partial, master, moment_one, moment_two, before, replicas):
    _, kinds, rows, half = partial.shape
    state = pl.BlockSpec((1, rows, half), lambda k, s: (k, 0, s[1]))

    def body(s, arrived_ref, partial_ref, master_ref, one_ref, two_ref, *refs):
        master_out, one_out, two_out = refs[-3:]
        summed = arrived_ref[0].astype(jnp.float32) + partial_ref[0, 0].astype(jnp.float32)
        grad_mean = summed / replicas
        one = beta_one * one_ref[0] + (1.0 - beta_one) * grad_mean
        two = beta_two * two_ref[0] + (1.0 - beta_two) * grad_mean * grad_mean
        old = master_ref[0]
        update = one / bias_one / (jnp.sqrt(two / bias_two) + adam_eps) + decay_rate * old
        master_out[0] = old - learn_rate * update
        one_out[0] = one
        two_out[0] = two

    aliases = {} if before is None else {6: 0, 7: 1, 8: 2}
    extra = () if before is None else before
    return pl.pallas_call(
        body,
        out_shape=(jax.ShapeDtypeStruct(master.shape, jnp.float32),) * 3,
        grid_spec=pltpu.PrefetchScalarGridSpec(
            num_scalar_prefetch=1,
            grid=(kinds,),
            in_specs=[
                pl.BlockSpec((1, rows, half), lambda k, s: (k, 0, 0)),
                pl.BlockSpec((1, 1, rows, half), lambda k, s: (s[0], k, 0, 0)),
                state,
                state,
                state,
            ]
            + [pl.BlockSpec(memory_space=pl.ANY)] * len(extra),
            out_specs=(state, state, state),
        ),
        input_output_aliases=aliases,
        cost_estimate=pl.CostEstimate(
            flops=20 * kinds * rows * half, bytes_accessed=28 * kinds * rows * half, transcendentals=0
        ),
        name="adam",
    )(place, arrived, partial, master, moment_one, moment_two, *extra)


def grouped(tokens, cotangent, working, degraded, block_map, master, moment_one, moment_two):
    replicas = lax.axis_size("dp")
    tp_size = lax.axis_size("tp")
    inner = 2 * CORES
    depth = replicas // inner
    me = lax.axis_index("tp")
    mine = lax.axis_index("dp")
    z, x, core = mine // inner, (mine // CORES) % 2, mine % CORES
    slot_count = working.shape[3] // BLOCK
    per_dev = BLOCKS // tp_size
    half = tokens.shape[1]

    tp_swap = [(i, (i + 1) % tp_size) for i in range(tp_size)]
    x_swap = [(i, i ^ CORES) for i in range(replicas)]
    core_swap = [(i, i ^ 1) for i in range(replicas)]

    def over_y(v):
        return lax.ppermute(v, "tp", tp_swap)

    def over_x(v):
        return lax.ppermute(v, "dp", x_swap)

    def over_core(v):
        return lax.ppermute(v, "dp", core_swap)

    def ring(v, step):
        return lax.ppermute(v, "dp", [(i, (i + step * inner) % replicas) for i in range(replicas)])

    order = jnp.arange(BLOCKS, dtype=jnp.int32)
    along = order % depth
    far_x = 1 - (order // depth) % 2
    far_y = 1 - order // per_dev
    block = ((me + far_y) % tp_size) * per_dev + along * 2 + (x ^ far_x)
    places = layout_places(degraded[0], block_map[0], tp_size, slot_count)
    blocks = jnp.arange(BLOCKS, dtype=jnp.int32)
    place = jnp.sum(jnp.where(block[:, None] == blocks[None, :], places[None, :], 0), axis=1)
    held = place // slot_count == me
    slots = jnp.where(held, place % slot_count, 0)
    extra = jnp.where(blocks == 0, me, jnp.where(blocks == 1, core, 0))
    scalars = jnp.concatenate([slots, held.astype(jnp.int32), extra.astype(jnp.int32)])

    t_own, c_own = tokens, cotangent
    t_other = over_y(t_own)
    t_own_x = over_x(t_own)
    t_other, c_first = lax.optimization_barrier((t_other, c_own))
    c_other = over_y(c_first)
    c_own_x = over_x(c_own)
    c_other, t_fwd, c_fwd = lax.optimization_barrier((c_other, t_other, c_own_x))
    t_other_x = over_x(t_fwd)
    c_other_x = over_y(c_fwd)
    own_t = [t_own, t_own_x, over_core(t_own), over_core(t_own_x)]
    own_c = [c_own, c_own_x, over_core(c_own), over_core(c_own_x)]
    other_t = [t_other, t_other_x, over_core(t_other), over_core(t_other_x)]
    other_c = [c_other, c_other_x, over_core(c_other), over_core(c_other_x)]

    gate, up = gate_up(scalars, t_own, t_other, working)
    theirs, far, near, grads = down_acts(scalars, c_own, c_other, working, gate, up)

    from_y = over_y(theirs)
    far = far + from_y[0]
    near = near + from_y[1]
    near_x = over_x(far)
    acts = [near, near_x, over_core(near[1]), over_core(near_x[1])]

    sent = over_y(input_part(scalars, grads, working, half, 1))
    kept = input_part(scalars, grads, working, half, 0)
    input_grad = (kept + sent.astype(jnp.float32)).astype(jnp.bfloat16)

    partials = [weight_grad(acts, own_t, own_c, replicas), weight_grad(acts, other_t, other_c, replicas)]
    steps = (1, -1)
    moving = [None, None]
    for s in range(1, depth):
        for h in range(2):
            chunk = lax.dynamic_index_in_dim(partials[h], (z - steps[h] * s) % depth, 0, keepdims=False)
            moving[h] = ring(chunk if moving[h] is None else chunk + moving[h], steps[h])
    state = None
    for h in range(2):
        where = jnp.stack([z, (me + h) % tp_size]).astype(jnp.int32)
        state = adam(where, moving[h], partials[h], master, moment_one, moment_two, state, replicas)
    return (input_grad, *state)


def solution(mesh):
    replicas, tp_size = mesh.shape["dp"], mesh.shape["tp"]
    inner = 2 * CORES

    def per_part(*args):
        half = args[0].shape[1]
        rows = args[5].shape[1]
        aligned = half % BLOCK == 0 and args[0].shape[0] % 16 == 0 and rows * CORES == BLOCK
        split = replicas % (2 * inner) == 0 and tp_size == 2 and BLOCKS == tp_size * replicas // CORES
        return (grouped if aligned and split else per_device)(*args)

    return jax.shard_map(
        per_part,
        mesh=mesh,
        in_specs=(
            P("dp", "tp"),
            P("dp", "tp"),
            P("dp", "tp", None, None, None),
            P("dp"),
            P("dp", None),
            P(None, ("tp", "dp"), None),
            P(None, ("tp", "dp"), None),
            P(None, ("tp", "dp"), None),
        ),
        out_specs=(
            P("dp", "tp"),
            P(None, ("tp", "dp"), None),
            P(None, ("tp", "dp"), None),
            P(None, ("tp", "dp"), None),
        ),
        check_vma=False,
    )
```

```python
import jax
import jax.numpy as jnp
from jax import lax
from jax.experimental import pallas as pl
from jax.experimental.pallas import tpu as pltpu
from jax.sharding import PartitionSpec as P

BLOCK = 128
BLOCKS = 16


beta_one = 0.9
beta_two = 0.95
learn_rate = 0.05
decay_rate = 0.1
adam_eps = 1e-08
bias_one = 1.0 - 0.9**10
bias_two = 1.0 - 0.95**10


def layout_places(replica_flag, mapping, tp_size, slot_count):
    blocks = jnp.arange(BLOCKS, dtype=jnp.int32)
    canonical = blocks // (BLOCKS // tp_size)
    holder = jnp.where(replica_flag > 0, mapping, canonical)
    earlier = (holder[None, :] == holder[:, None]) & (blocks[None, :] < blocks[:, None])
    slot_rank = jnp.sum(earlier.astype(jnp.int32), axis=1)
    return holder * slot_count + slot_rank


def per_device(tokens, cotangent, working, degraded, block_map, master, moment_one, moment_two):
    tp_size = lax.axis_size("tp")
    replicas = lax.axis_size("dp")
    my_index = lax.axis_index("tp")
    weights = working[0, 0]
    slot_count = weights.shape[1] // BLOCK
    per_dev = BLOCKS // tp_size
    places = layout_places(degraded[0], block_map[0], tp_size, slot_count)
    my_slots = my_index * slot_count + jnp.arange(slot_count, dtype=jnp.int32)
    holding = places[:, None] == my_slots[None, :]
    filled = jnp.any(holding, axis=0).astype(jnp.float32)
    column_mask = jnp.repeat(filled, BLOCK)
    inputs, upstream = (
        lax.all_gather(tokens, "tp", axis=1, tiled=True),
        lax.all_gather(cotangent, "tp", axis=1, tiled=True),
    )
    contract_d = (((1,), (1,)), ((), ()))
    gate_pre = lax.dot_general(inputs, weights[0], contract_d, preferred_element_type=jnp.float32)
    up_pre = lax.dot_general(inputs, weights[1], contract_d, preferred_element_type=jnp.float32)
    hidden_grad = lax.dot_general(
        upstream, weights[2], contract_d, preferred_element_type=jnp.float32
    )
    gate_sig = jax.nn.sigmoid(gate_pre)
    active = gate_pre * gate_sig
    hidden = (active * up_pre * column_mask).astype(jnp.bfloat16)
    gate_grad = (
        hidden_grad * up_pre * gate_sig * (1.0 + gate_pre * (1.0 - gate_sig)) * column_mask
    ).astype(jnp.bfloat16)
    up_grad = (hidden_grad * active * column_mask).astype(jnp.bfloat16)
    partial_value = jnp.dot(gate_grad, weights[0], preferred_element_type=jnp.float32) + jnp.dot(
        up_grad, weights[1], preferred_element_type=jnp.float32
    )
    input_grad = lax.psum_scatter(partial_value, "tp", scatter_dimension=1, tiled=True).astype(
        jnp.bfloat16
    )
    tok_rows = gate_grad.shape[0]
    packed = jnp.stack(
        [
            hidden.reshape(tok_rows, slot_count, BLOCK),
            gate_grad.reshape(tok_rows, slot_count, BLOCK),
            up_grad.reshape(tok_rows, slot_count, BLOCK),
        ],
        axis=2,
    )
    packed = packed.transpose(1, 0, 2, 3).reshape(slot_count, tok_rows, 3 * BLOCK)
    selector = holding.astype(jnp.bfloat16)
    outgoing = jnp.einsum(
        "qs,stc->qtc", selector, packed, preferred_element_type=jnp.float32
    ).astype(jnp.bfloat16)
    incoming = lax.all_to_all(outgoing, "tp", split_axis=0, concat_axis=0, tiled=True)
    owned_acts = jnp.sum(incoming.reshape(tp_size, per_dev, tok_rows, 3 * BLOCK), axis=0)
    owned_kinds = (
        owned_acts.reshape(per_dev, tok_rows, 3, BLOCK)
        .transpose(2, 1, 0, 3)
        .reshape(3, tok_rows, per_dev * BLOCK)
    )
    contract_t = (((0,), (0,)), ((), ()))
    gate_term = lax.dot_general(
        owned_kinds[1], inputs, contract_t, preferred_element_type=jnp.float32
    )
    up_term = lax.dot_general(
        owned_kinds[2], inputs, contract_t, preferred_element_type=jnp.float32
    )
    down_term = lax.dot_general(
        owned_kinds[0], upstream, contract_t, preferred_element_type=jnp.float32
    )
    summed = lax.psum_scatter(
        jnp.stack([gate_term, up_term, down_term], axis=1).astype(jnp.bfloat16),
        "dp",
        scatter_dimension=0,
        tiled=True,
    ).astype(jnp.float32)
    grad_mean = jnp.transpose(summed, (1, 0, 2)) / replicas
    moment_one_next = beta_one * moment_one + (1.0 - beta_one) * grad_mean
    moment_two_next = beta_two * moment_two + (1.0 - beta_two) * grad_mean * grad_mean
    update = (
        moment_one_next / bias_one / (jnp.sqrt(moment_two_next / bias_two) + adam_eps)
        + decay_rate * master
    )
    master_next = master - learn_rate * update
    return (input_grad, master_next, moment_one_next, moment_two_next)


CORES = 2
PAIR = 2
contract_last = (((1,), (1,)), ((), ()))
contract_mid = (((1,), (0,)), ((), ()))
contract_first = (((0,), (0,)), ((), ()))


def dot32(a, b, dims):
    return lax.dot_general(a, b, dims, preferred_element_type=jnp.float32)


def weight_specs(kinds, half, sides):
    specs = []
    for kind in kinds:
        for side in sides:
            for j in range(PAIR):

                def where(i, s, kind=kind, side=side, j=j):
                    column = s[2 * s.shape[0] // 3] if side == 0 else 1 - s[2 * s.shape[0] // 3]
                    return (0, 0, kind, s[PAIR * i + j], column)

                specs.append(pl.BlockSpec((1, 1, 1, BLOCK, half), where))
    return specs


def whole_spec(shape):
    return pl.BlockSpec(shape, lambda *_: (0,) * len(shape))


def both(first, second):
    return jnp.concatenate([first[0, 0, 0], second[0, 0, 0]], axis=0)


def own_part(scalars, tokens, cotangent, working):
    pairs = scalars.shape[0] // 6
    rows, half = tokens.shape

    def body(s, t_ref, c_ref, *refs):
        weights, outs = refs[:6], refs[6:]
        i = pl.program_id(0)

        @pl.when(s[2 * pairs + 2 * i] + s[2 * pairs + 2 * i + 1] > 0)
        def _():
            for kind, out in enumerate(outs):
                left = c_ref if kind == 2 else t_ref
                out[0] = dot32(left[...], both(*weights[2 * kind : 2 * kind + 2]), contract_last)

    out = jax.ShapeDtypeStruct((pairs, rows, PAIR * BLOCK), jnp.float32)
    return pl.pallas_call(
        body,
        out_shape=(out,) * 3,
        grid_spec=pltpu.PrefetchScalarGridSpec(
            num_scalar_prefetch=1,
            grid=(pairs,),
            in_specs=[whole_spec(tokens.shape)] * 2 + weight_specs((0, 1, 2), half, (0,)),
            out_specs=(pair_spec(rows),) * 3,
        ),
        cost_estimate=pl.CostEstimate(
            flops=6 * rows * half * pairs * PAIR * BLOCK,
            bytes_accessed=6 * half * pairs * PAIR * BLOCK,
            transcendentals=0,
        ),
        name="own_part",
    )(scalars, tokens, cotangent, *[working] * 6)


def pair_spec(rows):
    return pl.BlockSpec((1, rows, PAIR * BLOCK), lambda i, s: (i, 0, 0))


def act_outputs(pairs, kinds, rows):
    quarter = pairs // 4
    part = (quarter, kinds, rows, BLOCK)

    def theirs_at(i, s):
        at = jnp.minimum(i, 2 * quarter - 1)
        return (at // quarter, 0, at % quarter, 0, 0, 0)

    shapes = (
        jax.ShapeDtypeStruct((2, CORES, *part), jnp.bfloat16),
        jax.ShapeDtypeStruct((CORES, *part), jnp.bfloat16),
        jax.ShapeDtypeStruct((CORES, *part), jnp.bfloat16),
    )
    specs = (
        pl.BlockSpec((1, CORES, 1, kinds, rows, BLOCK), theirs_at),
        pl.BlockSpec(
            (CORES, 1, kinds, rows, BLOCK), lambda i, s: (0, jnp.clip(i - 2 * quarter, 0, quarter - 1), 0, 0, 0)
        ),
        pl.BlockSpec(
            (CORES, 1, kinds, rows, BLOCK), lambda i, s: (0, jnp.clip(i - 3 * quarter, 0, quarter - 1), 0, 0, 0)
        ),
    )
    return shapes, specs


def put_acts(i, pairs, core, values, theirs, far, near):
    quarter = pairs // 4
    narrow = BLOCK // CORES
    pieces = [
        [
            jnp.concatenate(
                [value[:, j * BLOCK + c * narrow : j * BLOCK + (c + 1) * narrow] for j in range(PAIR)], axis=1
            ).astype(jnp.bfloat16)
            for c in range(CORES)
        ]
        for value in values
    ]
    slots = [jnp.bitwise_xor(core, c) for c in range(CORES)]

    @pl.when(i < 2 * quarter)
    def _():
        for kind, piece in enumerate(pieces):
            for c in range(CORES):
                theirs[0, slots[c], 0, kind] = piece[c]

    for ref, low in ((far, 2 * quarter), (near, 3 * quarter)):

        @pl.when((i >= low) & (i < low + quarter))
        def _(ref=ref):
            for kind, piece in enumerate(pieces):
                for c in range(CORES):
                    ref[slots[c], 0, kind] = piece[c]


def gate_up(scalars, other, working, gate, up):
    pairs = scalars.shape[0] // 6
    rows, half = other.shape

    def body(s, other_ref, w0, w1, w2, w3, gate_ref, up_ref, act_ref, slope_ref, *outs):
        i = pl.program_id(0)
        has = [s[2 * pairs + 2 * i + j] for j in range(PAIR)]
        core = s[4 * pairs + 1]

        @pl.when(has[0] + has[1] > 0)
        def _():
            zg = gate_ref[0] + dot32(other_ref[...], both(w0, w1), contract_last)
            zu = up_ref[0] + dot32(other_ref[...], both(w2, w3), contract_last)
            lane = lax.broadcasted_iota(jnp.int32, zg.shape, 1)
            keep = jnp.where(lane < BLOCK, has[0], has[1]) > 0
            sig = jax.nn.sigmoid(zg)
            act = zg * sig
            act_ref[0] = act
            slope_ref[0] = zu * sig * (1.0 + zg * (1.0 - sig))
            put_acts(i, pairs, core, [jnp.where(keep, act * zu, 0.0)], *outs)

        @pl.when(has[0] + has[1] == 0)
        def _():
            put_acts(i, pairs, core, [jnp.zeros((rows, PAIR * BLOCK), jnp.float32)], *outs)

    out = jax.ShapeDtypeStruct((pairs, rows, PAIR * BLOCK), jnp.float32)
    shapes, specs = act_outputs(pairs, 1, rows)
    return pl.pallas_call(
        body,
        out_shape=(out, out, *shapes),
        grid_spec=pltpu.PrefetchScalarGridSpec(
            num_scalar_prefetch=1,
            grid=(pairs,),
            in_specs=[whole_spec(other.shape)] + weight_specs((0, 1), half, (1,)) + [pair_spec(rows)] * 2,
            out_specs=(pair_spec(rows), pair_spec(rows), *specs),
        ),
        cost_estimate=pl.CostEstimate(
            flops=4 * rows * half * pairs * PAIR * BLOCK,
            bytes_accessed=4 * half * pairs * PAIR * BLOCK + 16 * rows * pairs * PAIR * BLOCK,
            transcendentals=rows * pairs * PAIR * BLOCK,
        ),
        name="gate_up",
    )(scalars, other, *[working] * 4, gate, up)


def down_acts(scalars, other, working, partial, act, slope):
    pairs = scalars.shape[0] // 6
    rows, half = other.shape

    def body(s, other_ref, w0, w1, partial_ref, act_ref, slope_ref, grads, *outs):
        i = pl.program_id(0)
        has = [s[2 * pairs + 2 * i + j] for j in range(PAIR)]
        core = s[4 * pairs + 1]

        @pl.when(has[0] + has[1] > 0)
        def _():
            dh = partial_ref[0] + dot32(other_ref[...], both(w0, w1), contract_last)
            lane = lax.broadcasted_iota(jnp.int32, dh.shape, 1)
            keep = jnp.where(lane < BLOCK, has[0], has[1]) > 0
            dgate = jnp.where(keep, dh * slope_ref[0], 0.0)
            dup = jnp.where(keep, dh * act_ref[0], 0.0)
            grads[0, 0] = dgate.astype(jnp.bfloat16)
            grads[0, 1] = dup.astype(jnp.bfloat16)
            put_acts(i, pairs, core, [dgate, dup], *outs)

        @pl.when(has[0] + has[1] == 0)
        def _():
            zero = jnp.zeros((rows, PAIR * BLOCK), jnp.float32)
            grads[...] = jnp.zeros(grads.shape, grads.dtype)
            put_acts(i, pairs, core, [zero, zero], *outs)

    shapes, specs = act_outputs(pairs, 2, rows)
    return pl.pallas_call(
        body,
        out_shape=(jax.ShapeDtypeStruct((pairs, 2, rows, PAIR * BLOCK), jnp.bfloat16), *shapes),
        grid_spec=pltpu.PrefetchScalarGridSpec(
            num_scalar_prefetch=1,
            grid=(pairs,),
            in_specs=[whole_spec(other.shape)] + weight_specs((2,), half, (1,)) + [pair_spec(rows)] * 3,
            out_specs=(pl.BlockSpec((1, 2, rows, PAIR * BLOCK), lambda i, s: (i, 0, 0, 0)), *specs),
        ),
        cost_estimate=pl.CostEstimate(
            flops=2 * rows * half * pairs * PAIR * BLOCK,
            bytes_accessed=2 * half * pairs * PAIR * BLOCK + 20 * rows * pairs * PAIR * BLOCK,
            transcendentals=0,
        ),
        name="down_acts",
    )(scalars, other, *[working] * 2, partial, act, slope)


def input_part(scalars, grads, working, half, side):
    pairs = scalars.shape[0] // 6
    rows = grads.shape[2]

    def body(s, grads_ref, w0, w1, w2, w3, out_ref, total):
        i = pl.program_id(0)

        @pl.when(i == 0)
        def _():
            total[...] = jnp.zeros(total.shape, total.dtype)

        @pl.when(s[2 * pairs + 2 * i] + s[2 * pairs + 2 * i + 1] > 0)
        def _():
            total[...] += dot32(grads_ref[0, 0], both(w0, w1), contract_mid) + dot32(
                grads_ref[0, 1], both(w2, w3), contract_mid
            )

        @pl.when(i == pairs - 1)
        def _():
            out_ref[...] = total[...].astype(out_ref.dtype)

    return pl.pallas_call(
        body,
        out_shape=jax.ShapeDtypeStruct((rows, half), jnp.bfloat16 if side else jnp.float32),
        grid_spec=pltpu.PrefetchScalarGridSpec(
            num_scalar_prefetch=1,
            grid=(pairs,),
            in_specs=[pl.BlockSpec((1, 2, rows, PAIR * BLOCK), lambda i, s: (i, 0, 0, 0))]
            + weight_specs((0, 1), half, (side,)),
            out_specs=whole_spec((rows, half)),
            scratch_shapes=[pltpu.VMEM((rows, half), jnp.float32)],
        ),
        cost_estimate=pl.CostEstimate(
            flops=4 * rows * half * pairs * PAIR * BLOCK,
            bytes_accessed=4 * half * pairs * PAIR * BLOCK,
            transcendentals=0,
        ),
        name="input_other" if side else "input_own",
    )(scalars, grads, *[working] * 4)


def weight_grad(acts, inputs, name):
    group = len(acts)
    quarter, kinds, rows, _ = acts[0].shape[-4:]
    half = inputs[0].shape[1]
    narrow = BLOCK // CORES
    wide = quarter * BLOCK
    tile = half // 2 if half % (2 * BLOCK) == 0 else half

    def body(*refs):
        a_refs, x_refs = refs[:group], refs[group : 2 * group]
        out_ref, left = refs[2 * group :]

        @pl.when(pl.program_id(0) == 0)
        def _():
            for kind in range(kinds):
                for p in range(quarter):
                    column = jnp.concatenate(
                        [ref[0, p, kind] if len(ref.shape) == 5 else ref[p, kind] for ref in a_refs], axis=0
                    )
                    left[kind, p * BLOCK : (p + 1) * BLOCK, :] = column.T

        right = jnp.concatenate([ref[...] for ref in x_refs], axis=0)
        for kind in range(kinds):
            value = dot32(left[kind], right, contract_mid).astype(jnp.bfloat16)
            for z in range(2 * quarter):
                out_ref[z, kind] = value[z * narrow : (z + 1) * narrow]

    def act_spec(a):
        if a.ndim == 5:
            return pl.BlockSpec((1, *a.shape[1:]), lambda i: (0,) * 5)
        return pl.BlockSpec(a.shape, lambda i: (0,) * 4)

    return pl.pallas_call(
        body,
        out_shape=jax.ShapeDtypeStruct((2 * quarter, kinds, narrow, half), jnp.bfloat16),
        grid=(half // tile,),
        in_specs=[act_spec(a) for a in acts] + [pl.BlockSpec((rows, tile), lambda i: (0, i))] * group,
        out_specs=pl.BlockSpec((2 * quarter, kinds, narrow, tile), lambda i: (0, 0, 0, i)),
        scratch_shapes=[pltpu.VMEM((kinds, wide, group * rows), jnp.bfloat16)],
        cost_estimate=pl.CostEstimate(
            flops=2 * kinds * group * rows * wide * half,
            bytes_accessed=2 * group * rows * half + 2 * kinds * wide * half,
            transcendentals=0,
        ),
        name=name,
    )(*acts, *inputs)


def adam(place, arrived, partial, first, master, moment_one, moment_two, before, replicas):
    _, kinds, rows, half = partial.shape
    step = 16 if rows % 16 == 0 else rows
    state = pl.BlockSpec((1, step, half), lambda k, i, s: (k + first, i, s[1]))

    def body(s, arrived_ref, partial_ref, master_ref, one_ref, two_ref, *refs):
        master_out, one_out, two_out = refs[-3:]
        summed = arrived_ref[0].astype(jnp.float32) + partial_ref[0, 0].astype(jnp.float32)
        grad_mean = summed * (1.0 / replicas)
        one = beta_one * one_ref[0] + (1.0 - beta_one) * grad_mean
        two = beta_two * two_ref[0] + (1.0 - beta_two) * grad_mean * grad_mean
        old = master_ref[0]
        update = one * (1.0 / bias_one) / (jnp.sqrt(two * (1.0 / bias_two)) + adam_eps) + decay_rate * old
        master_out[0] = old - learn_rate * update
        one_out[0] = one
        two_out[0] = two

    aliases = {} if before is None else {6: 0, 7: 1, 8: 2}
    extra = () if before is None else before
    return pl.pallas_call(
        body,
        out_shape=(jax.ShapeDtypeStruct(master.shape, jnp.float32),) * 3,
        grid_spec=pltpu.PrefetchScalarGridSpec(
            num_scalar_prefetch=1,
            grid=(kinds, rows // step),
            in_specs=[
                pl.BlockSpec((1, step, half), lambda k, i, s: (k, i, 0)),
                pl.BlockSpec((1, 1, step, half), lambda k, i, s: (s[0], k, i, 0)),
                state,
                state,
                state,
            ]
            + [pl.BlockSpec(memory_space=pl.ANY)] * len(extra),
            out_specs=(state, state, state),
        ),
        input_output_aliases=aliases,
        cost_estimate=pl.CostEstimate(
            flops=20 * kinds * rows * half, bytes_accessed=28 * kinds * rows * half, transcendentals=0
        ),
        name="adam",
    )(place, arrived, partial, master, moment_one, moment_two, *extra)


def grouped(tokens, cotangent, working, degraded, block_map, master, moment_one, moment_two):
    replicas = lax.axis_size("dp")
    tp_size = lax.axis_size("tp")
    inner = 2 * CORES
    depth = replicas // inner
    me = lax.axis_index("tp")
    mine = lax.axis_index("dp")
    z, x, core = mine // inner, (mine // CORES) % 2, mine % CORES
    slot_count = working.shape[3] // BLOCK
    per_dev = BLOCKS // tp_size
    half = tokens.shape[1]

    tp_swap = [(i, (i + 1) % tp_size) for i in range(tp_size)]
    x_swap = [(i, i ^ CORES) for i in range(replicas)]
    core_swap = [(i, i ^ 1) for i in range(replicas)]
    after = lax.optimization_barrier

    def over_y(v):
        return lax.ppermute(v, "tp", tp_swap)

    def over_x(v):
        return lax.ppermute(v, "dp", x_swap)

    def over_core(v):
        return lax.ppermute(v, "dp", core_swap)

    def ring(v, step):
        return lax.ppermute(v, "dp", [(i, (i + step * inner) % replicas) for i in range(replicas)])

    order = jnp.arange(BLOCKS, dtype=jnp.int32)
    along = order % depth
    far_x = 1 - (order // depth) % 2
    far_y = 1 - order // per_dev
    block = ((me + far_y) % tp_size) * per_dev + along * 2 + (x ^ far_x)
    places = layout_places(degraded[0], block_map[0], tp_size, slot_count)
    blocks = jnp.arange(BLOCKS, dtype=jnp.int32)
    place = jnp.sum(jnp.where(block[:, None] == blocks[None, :], places[None, :], 0), axis=1)
    held = place // slot_count == me
    slots = jnp.where(held, place % slot_count, 0)
    extra = jnp.where(blocks == 0, me, jnp.where(blocks == 1, core, 0))
    scalars = jnp.concatenate([slots, held.astype(jnp.int32), extra.astype(jnp.int32)])

    t_own, c_own = tokens, cotangent
    t_other = over_y(t_own)
    c_own_x = over_x(c_own)
    t_own_x = over_x(t_own)
    gate, up, down = own_part(scalars, t_own, c_own, working)
    t_other, c_first = after((t_other, c_own))
    c_other = over_y(c_first)
    act, slope, h_theirs, h_far, h_near = gate_up(scalars, t_other, working, gate, up)
    c_other, h_theirs = after((c_other, h_theirs))
    h_from = over_y(h_theirs)
    c_other_x = over_x(c_other)
    grads, d_theirs, d_far, d_near = down_acts(scalars, c_other, working, down, act, slope)
    h_from, d_theirs = after((h_from, d_theirs))
    d_from = over_y(d_theirs)

    def exchange(own, own_x):
        return [own, own_x, over_core(own), over_core(own_x)]

    def spread(far, near, came):
        near_x = over_x(far + came[0])
        near = near + came[1]
        return [near, near_x, over_core(near[1]), over_core(near_x[1])]

    hidden_acts = spread(h_far, h_near, h_from)
    c_acts = [exchange(c_own, c_own_x), exchange(c_other, c_other_x)]
    hidden_acts[1], t_late = after((hidden_acts[1], t_other))
    t_other_x = over_x(t_late)
    t_acts = [exchange(t_own, t_own_x), exchange(t_other, t_other_x)]

    parts = [(2, h, weight_grad(hidden_acts, c_acts[h], "grad_down")) for h in range(2)]
    grad_acts = spread(d_far, d_near, d_from)
    parts += [(0, h, weight_grad(grad_acts, t_acts[h], "grad_up")) for h in range(2)]
    steps = (1, -1)
    moving = [None] * len(parts)
    for low in (0, 2):
        for s in range(1, depth):
            for at in (low, low + 1):
                _, h, partial = parts[at]
                chunk = lax.dynamic_index_in_dim(partial, (z - steps[h] * s) % depth, 0, keepdims=False)
                moving[at] = ring(chunk if moving[at] is None else chunk + moving[at], steps[h])

    sent = over_y(input_part(scalars, grads, working, half, 1))
    kept = input_part(scalars, grads, working, half, 0)
    input_grad = (kept + sent.astype(jnp.float32)).astype(jnp.bfloat16)

    state = None
    for (first, h, partial), arrived in zip(parts, moving):
        where = jnp.stack([z, (me + h) % tp_size]).astype(jnp.int32)
        state = adam(where, arrived, partial, first, master, moment_one, moment_two, state, replicas)
    return (input_grad, *state)


def solution(mesh):
    replicas, tp_size = mesh.shape["dp"], mesh.shape["tp"]
    inner = 2 * CORES

    def per_part(*args):
        half = args[0].shape[1]
        rows = args[5].shape[1]
        aligned = half % BLOCK == 0 and args[0].shape[0] % 16 == 0 and rows * CORES == BLOCK
        split = replicas % (2 * inner) == 0 and tp_size == 2 and BLOCKS == tp_size * replicas // CORES
        return (grouped if aligned and split else per_device)(*args)

    return jax.shard_map(
        per_part,
        mesh=mesh,
        in_specs=(
            P("dp", "tp"),
            P("dp", "tp"),
            P("dp", "tp", None, None, None),
            P("dp"),
            P("dp", None),
            P(None, ("tp", "dp"), None),
            P(None, ("tp", "dp"), None),
            P(None, ("tp", "dp"), None),
        ),
        out_specs=(
            P("dp", "tp"),
            P(None, ("tp", "dp"), None),
            P(None, ("tp", "dp"), None),
            P(None, ("tp", "dp"), None),
        ),
        check_vma=False,
    )
```

```python
import jax
import jax.numpy as jnp
from jax import lax
from jax.experimental import pallas as pl
from jax.experimental.pallas import tpu as pltpu
from jax.sharding import PartitionSpec as P

BLOCK = 128
BLOCKS = 16


beta_one = 0.9
beta_two = 0.95
learn_rate = 0.05
decay_rate = 0.1
adam_eps = 1e-08
bias_one = 1.0 - 0.9**10
bias_two = 1.0 - 0.95**10


def layout_places(replica_flag, mapping, tp_size, slot_count):
    blocks = jnp.arange(BLOCKS, dtype=jnp.int32)
    canonical = blocks // (BLOCKS // tp_size)
    holder = jnp.where(replica_flag > 0, mapping, canonical)
    earlier = (holder[None, :] == holder[:, None]) & (blocks[None, :] < blocks[:, None])
    slot_rank = jnp.sum(earlier.astype(jnp.int32), axis=1)
    return holder * slot_count + slot_rank


def per_device(tokens, cotangent, working, degraded, block_map, master, moment_one, moment_two):
    tp_size = lax.axis_size("tp")
    replicas = lax.axis_size("dp")
    my_index = lax.axis_index("tp")
    weights = working[0, 0]
    slot_count = weights.shape[1] // BLOCK
    per_dev = BLOCKS // tp_size
    places = layout_places(degraded[0], block_map[0], tp_size, slot_count)
    my_slots = my_index * slot_count + jnp.arange(slot_count, dtype=jnp.int32)
    holding = places[:, None] == my_slots[None, :]
    filled = jnp.any(holding, axis=0).astype(jnp.float32)
    column_mask = jnp.repeat(filled, BLOCK)
    inputs, upstream = (
        lax.all_gather(tokens, "tp", axis=1, tiled=True),
        lax.all_gather(cotangent, "tp", axis=1, tiled=True),
    )
    contract_d = (((1,), (1,)), ((), ()))
    gate_pre = lax.dot_general(inputs, weights[0], contract_d, preferred_element_type=jnp.float32)
    up_pre = lax.dot_general(inputs, weights[1], contract_d, preferred_element_type=jnp.float32)
    hidden_grad = lax.dot_general(
        upstream, weights[2], contract_d, preferred_element_type=jnp.float32
    )
    gate_sig = jax.nn.sigmoid(gate_pre)
    active = gate_pre * gate_sig
    hidden = (active * up_pre * column_mask).astype(jnp.bfloat16)
    gate_grad = (
        hidden_grad * up_pre * gate_sig * (1.0 + gate_pre * (1.0 - gate_sig)) * column_mask
    ).astype(jnp.bfloat16)
    up_grad = (hidden_grad * active * column_mask).astype(jnp.bfloat16)
    partial_value = jnp.dot(gate_grad, weights[0], preferred_element_type=jnp.float32) + jnp.dot(
        up_grad, weights[1], preferred_element_type=jnp.float32
    )
    input_grad = lax.psum_scatter(partial_value, "tp", scatter_dimension=1, tiled=True).astype(
        jnp.bfloat16
    )
    tok_rows = gate_grad.shape[0]
    packed = jnp.stack(
        [
            hidden.reshape(tok_rows, slot_count, BLOCK),
            gate_grad.reshape(tok_rows, slot_count, BLOCK),
            up_grad.reshape(tok_rows, slot_count, BLOCK),
        ],
        axis=2,
    )
    packed = packed.transpose(1, 0, 2, 3).reshape(slot_count, tok_rows, 3 * BLOCK)
    selector = holding.astype(jnp.bfloat16)
    outgoing = jnp.einsum(
        "qs,stc->qtc", selector, packed, preferred_element_type=jnp.float32
    ).astype(jnp.bfloat16)
    incoming = lax.all_to_all(outgoing, "tp", split_axis=0, concat_axis=0, tiled=True)
    owned_acts = jnp.sum(incoming.reshape(tp_size, per_dev, tok_rows, 3 * BLOCK), axis=0)
    owned_kinds = (
        owned_acts.reshape(per_dev, tok_rows, 3, BLOCK)
        .transpose(2, 1, 0, 3)
        .reshape(3, tok_rows, per_dev * BLOCK)
    )
    contract_t = (((0,), (0,)), ((), ()))
    gate_term = lax.dot_general(
        owned_kinds[1], inputs, contract_t, preferred_element_type=jnp.float32
    )
    up_term = lax.dot_general(
        owned_kinds[2], inputs, contract_t, preferred_element_type=jnp.float32
    )
    down_term = lax.dot_general(
        owned_kinds[0], upstream, contract_t, preferred_element_type=jnp.float32
    )
    summed = lax.psum_scatter(
        jnp.stack([gate_term, up_term, down_term], axis=1).astype(jnp.bfloat16),
        "dp",
        scatter_dimension=0,
        tiled=True,
    ).astype(jnp.float32)
    grad_mean = jnp.transpose(summed, (1, 0, 2)) / replicas
    moment_one_next = beta_one * moment_one + (1.0 - beta_one) * grad_mean
    moment_two_next = beta_two * moment_two + (1.0 - beta_two) * grad_mean * grad_mean
    update = (
        moment_one_next / bias_one / (jnp.sqrt(moment_two_next / bias_two) + adam_eps)
        + decay_rate * master
    )
    master_next = master - learn_rate * update
    return (input_grad, master_next, moment_one_next, moment_two_next)


CORES = 2
PAIR = 2
contract_last = (((1,), (1,)), ((), ()))
contract_mid = (((1,), (0,)), ((), ()))


def dot32(a, b, dims):
    return lax.dot_general(a, b, dims, preferred_element_type=jnp.float32)


def weight_specs(kinds, half, sides):
    specs = []
    for kind in kinds:
        for side in sides:
            for j in range(PAIR):

                def where(i, s, kind=kind, side=side, j=j):
                    column = s[2 * s.shape[0] // 3] if side == 0 else 1 - s[2 * s.shape[0] // 3]
                    return (0, 0, kind, s[PAIR * i + j], column)

                specs.append(pl.BlockSpec((1, 1, 1, BLOCK, half), where))
    return specs


def whole_spec(shape):
    return pl.BlockSpec(shape, lambda *_: (0,) * len(shape))


def both(first, second):
    return jnp.concatenate([first[0, 0, 0], second[0, 0, 0]], axis=0)


def own_part(scalars, tokens, cotangent, working):
    pairs = scalars.shape[0] // 6
    rows, half = tokens.shape

    def body(s, t_ref, c_ref, *refs):
        weights, outs = refs[:6], refs[6:]
        i = pl.program_id(0)

        @pl.when(s[2 * pairs + 2 * i] + s[2 * pairs + 2 * i + 1] > 0)
        def _():
            for kind, out in enumerate(outs):
                left = c_ref if kind == 2 else t_ref
                out[0] = dot32(left[...], both(*weights[2 * kind : 2 * kind + 2]), contract_last)

    out = jax.ShapeDtypeStruct((pairs, rows, PAIR * BLOCK), jnp.float32)
    return pl.pallas_call(
        body,
        out_shape=(out,) * 3,
        grid_spec=pltpu.PrefetchScalarGridSpec(
            num_scalar_prefetch=1,
            grid=(pairs,),
            in_specs=[whole_spec(tokens.shape)] * 2 + weight_specs((0, 1, 2), half, (0,)),
            out_specs=(pair_spec(rows),) * 3,
        ),
        cost_estimate=pl.CostEstimate(
            flops=6 * rows * half * pairs * PAIR * BLOCK,
            bytes_accessed=6 * half * pairs * PAIR * BLOCK,
            transcendentals=0,
        ),
        name="own_part",
    )(scalars, tokens, cotangent, *[working] * 6)


def pair_spec(rows):
    return pl.BlockSpec((1, rows, PAIR * BLOCK), lambda i, s: (i, 0, 0))


def act_outputs(pairs, kinds, rows):
    quarter = pairs // 4
    part = (quarter, kinds, rows, BLOCK)

    def theirs_at(i, s):
        at = jnp.minimum(i, 2 * quarter - 1)
        return (at // quarter, 0, at % quarter, 0, 0, 0)

    shapes = (
        jax.ShapeDtypeStruct((2, CORES, *part), jnp.bfloat16),
        jax.ShapeDtypeStruct((CORES, *part), jnp.bfloat16),
        jax.ShapeDtypeStruct((CORES, *part), jnp.bfloat16),
    )
    specs = (
        pl.BlockSpec((1, CORES, 1, kinds, rows, BLOCK), theirs_at),
        pl.BlockSpec(
            (CORES, 1, kinds, rows, BLOCK), lambda i, s: (0, jnp.clip(i - 2 * quarter, 0, quarter - 1), 0, 0, 0)
        ),
        pl.BlockSpec(
            (CORES, 1, kinds, rows, BLOCK), lambda i, s: (0, jnp.clip(i - 3 * quarter, 0, quarter - 1), 0, 0, 0)
        ),
    )
    return shapes, specs


def put_acts(i, pairs, core, values, theirs, far, near):
    quarter = pairs // 4
    narrow = BLOCK // CORES
    pieces = [
        [
            jnp.concatenate(
                [value[:, j * BLOCK + c * narrow : j * BLOCK + (c + 1) * narrow] for j in range(PAIR)], axis=1
            ).astype(jnp.bfloat16)
            for c in range(CORES)
        ]
        for value in values
    ]
    slots = [jnp.bitwise_xor(core, c) for c in range(CORES)]

    @pl.when(i < 2 * quarter)
    def _():
        for kind, piece in enumerate(pieces):
            for c in range(CORES):
                theirs[0, slots[c], 0, kind] = piece[c]

    for ref, low in ((far, 2 * quarter), (near, 3 * quarter)):

        @pl.when((i >= low) & (i < low + quarter))
        def _(ref=ref):
            for kind, piece in enumerate(pieces):
                for c in range(CORES):
                    ref[slots[c], 0, kind] = piece[c]


def gate_up(scalars, other, working, gate, up):
    pairs = scalars.shape[0] // 6
    rows, half = other.shape

    def body(s, other_ref, w0, w1, w2, w3, gate_ref, up_ref, act_ref, slope_ref, *outs):
        i = pl.program_id(0)
        has = [s[2 * pairs + 2 * i + j] for j in range(PAIR)]
        core = s[4 * pairs + 1]

        @pl.when(has[0] + has[1] > 0)
        def _():
            zg = gate_ref[0] + dot32(other_ref[...], both(w0, w1), contract_last)
            zu = up_ref[0] + dot32(other_ref[...], both(w2, w3), contract_last)
            lane = lax.broadcasted_iota(jnp.int32, zg.shape, 1)
            keep = jnp.where(lane < BLOCK, has[0], has[1]) > 0
            sig = jax.nn.sigmoid(zg)
            act = zg * sig
            act_ref[0] = act
            slope_ref[0] = zu * sig * (1.0 + zg * (1.0 - sig))
            put_acts(i, pairs, core, [jnp.where(keep, act * zu, 0.0)], *outs)

        @pl.when(has[0] + has[1] == 0)
        def _():
            put_acts(i, pairs, core, [jnp.zeros((rows, PAIR * BLOCK), jnp.float32)], *outs)

    out = jax.ShapeDtypeStruct((pairs, rows, PAIR * BLOCK), jnp.float32)
    shapes, specs = act_outputs(pairs, 1, rows)
    return pl.pallas_call(
        body,
        out_shape=(out, out, *shapes),
        grid_spec=pltpu.PrefetchScalarGridSpec(
            num_scalar_prefetch=1,
            grid=(pairs,),
            in_specs=[whole_spec(other.shape)] + weight_specs((0, 1), half, (1,)) + [pair_spec(rows)] * 2,
            out_specs=(pair_spec(rows), pair_spec(rows), *specs),
        ),
        cost_estimate=pl.CostEstimate(
            flops=4 * rows * half * pairs * PAIR * BLOCK,
            bytes_accessed=4 * half * pairs * PAIR * BLOCK + 16 * rows * pairs * PAIR * BLOCK,
            transcendentals=rows * pairs * PAIR * BLOCK,
        ),
        name="gate_up",
    )(scalars, other, *[working] * 4, gate, up)


def down_acts(scalars, other, working, partial, act, slope):
    pairs = scalars.shape[0] // 6
    rows, half = other.shape

    def body(s, other_ref, w0, w1, partial_ref, act_ref, slope_ref, grads, *outs):
        i = pl.program_id(0)
        has = [s[2 * pairs + 2 * i + j] for j in range(PAIR)]
        core = s[4 * pairs + 1]

        @pl.when(has[0] + has[1] > 0)
        def _():
            dh = partial_ref[0] + dot32(other_ref[...], both(w0, w1), contract_last)
            lane = lax.broadcasted_iota(jnp.int32, dh.shape, 1)
            keep = jnp.where(lane < BLOCK, has[0], has[1]) > 0
            dgate = jnp.where(keep, dh * slope_ref[0], 0.0)
            dup = jnp.where(keep, dh * act_ref[0], 0.0)
            grads[0, 0] = dgate.astype(jnp.bfloat16)
            grads[0, 1] = dup.astype(jnp.bfloat16)
            put_acts(i, pairs, core, [dgate, dup], *outs)

        @pl.when(has[0] + has[1] == 0)
        def _():
            zero = jnp.zeros((rows, PAIR * BLOCK), jnp.float32)
            grads[...] = jnp.zeros(grads.shape, grads.dtype)
            put_acts(i, pairs, core, [zero, zero], *outs)

    shapes, specs = act_outputs(pairs, 2, rows)
    return pl.pallas_call(
        body,
        out_shape=(jax.ShapeDtypeStruct((pairs, 2, rows, PAIR * BLOCK), jnp.bfloat16), *shapes),
        grid_spec=pltpu.PrefetchScalarGridSpec(
            num_scalar_prefetch=1,
            grid=(pairs,),
            in_specs=[whole_spec(other.shape)] + weight_specs((2,), half, (1,)) + [pair_spec(rows)] * 3,
            out_specs=(pl.BlockSpec((1, 2, rows, PAIR * BLOCK), lambda i, s: (i, 0, 0, 0)), *specs),
        ),
        cost_estimate=pl.CostEstimate(
            flops=2 * rows * half * pairs * PAIR * BLOCK,
            bytes_accessed=2 * half * pairs * PAIR * BLOCK + 20 * rows * pairs * PAIR * BLOCK,
            transcendentals=0,
        ),
        name="down_acts",
    )(scalars, other, *[working] * 2, partial, act, slope)


def input_part(scalars, grads, working, half, side):
    pairs = scalars.shape[0] // 6
    rows = grads.shape[2]

    def body(s, grads_ref, w0, w1, w2, w3, out_ref, total):
        i = pl.program_id(0)

        @pl.when(i == 0)
        def _():
            total[...] = jnp.zeros(total.shape, total.dtype)

        @pl.when(s[2 * pairs + 2 * i] + s[2 * pairs + 2 * i + 1] > 0)
        def _():
            total[...] += dot32(grads_ref[0, 0], both(w0, w1), contract_mid) + dot32(
                grads_ref[0, 1], both(w2, w3), contract_mid
            )

        @pl.when(i == pairs - 1)
        def _():
            out_ref[...] = total[...].astype(out_ref.dtype)

    return pl.pallas_call(
        body,
        out_shape=jax.ShapeDtypeStruct((rows, half), jnp.bfloat16 if side else jnp.float32),
        grid_spec=pltpu.PrefetchScalarGridSpec(
            num_scalar_prefetch=1,
            grid=(pairs,),
            in_specs=[pl.BlockSpec((1, 2, rows, PAIR * BLOCK), lambda i, s: (i, 0, 0, 0))]
            + weight_specs((0, 1), half, (side,)),
            out_specs=whole_spec((rows, half)),
            scratch_shapes=[pltpu.VMEM((rows, half), jnp.float32)],
        ),
        cost_estimate=pl.CostEstimate(
            flops=4 * rows * half * pairs * PAIR * BLOCK,
            bytes_accessed=4 * half * pairs * PAIR * BLOCK,
            transcendentals=0,
        ),
        name="input_other" if side else "input_own",
    )(scalars, grads, *[working] * 4)


def weight_grad(acts, inputs):
    group = len(acts)
    quarter, kinds, rows, _ = acts[0].shape[-4:]
    half = inputs[0].shape[1]
    narrow = BLOCK // CORES
    wide = quarter * BLOCK
    tile = half // 2 if half % (2 * BLOCK) == 0 else half

    def body(*refs):
        a_refs, x_refs = refs[:group], refs[group : 2 * group]
        out_ref, left = refs[2 * group :]

        @pl.when(pl.program_id(0) == 0)
        def _():
            for kind in range(kinds):
                for p in range(quarter):
                    column = jnp.concatenate(
                        [ref[0, p, kind] if len(ref.shape) == 5 else ref[p, kind] for ref in a_refs], axis=0
                    )
                    left[kind, p * BLOCK : (p + 1) * BLOCK, :] = column.T

        right = jnp.concatenate([ref[...] for ref in x_refs], axis=0)
        for kind in range(kinds):
            value = dot32(left[kind], right, contract_mid).astype(jnp.bfloat16)
            for z in range(2 * quarter):
                out_ref[z, kind] = value[z * narrow : (z + 1) * narrow]

    def act_spec(a):
        if a.ndim == 5:
            return pl.BlockSpec((1, *a.shape[1:]), lambda i: (0,) * 5)
        return pl.BlockSpec(a.shape, lambda i: (0,) * 4)

    return pl.pallas_call(
        body,
        out_shape=jax.ShapeDtypeStruct((2 * quarter, kinds, narrow, half), jnp.bfloat16),
        grid=(half // tile,),
        in_specs=[act_spec(a) for a in acts] + [pl.BlockSpec((rows, tile), lambda i: (0, i))] * group,
        out_specs=pl.BlockSpec((2 * quarter, kinds, narrow, tile), lambda i: (0, 0, 0, i)),
        scratch_shapes=[pltpu.VMEM((kinds, wide, group * rows), jnp.bfloat16)],
        cost_estimate=pl.CostEstimate(
            flops=2 * kinds * group * rows * wide * half,
            bytes_accessed=2 * group * rows * half + 2 * kinds * wide * half,
            transcendentals=0,
        ),
    )(*acts, *inputs)


def adam(place, arrived, partial, first, master, moment_one, moment_two, before, replicas):
    _, kinds, rows, half = partial.shape
    step = rows
    state = pl.BlockSpec((1, step, half), lambda k, i, s: (k + first, i, s[1]))

    def body(s, arrived_ref, partial_ref, master_ref, one_ref, two_ref, *refs):
        master_out, one_out, two_out = refs[-3:]
        summed = arrived_ref[0].astype(jnp.float32) + partial_ref[0, 0].astype(jnp.float32)
        grad_mean = summed * (1.0 / replicas)
        one = beta_one * one_ref[0] + (1.0 - beta_one) * grad_mean
        two = beta_two * two_ref[0] + (1.0 - beta_two) * grad_mean * grad_mean
        old = master_ref[0]
        update = one * (1.0 / bias_one) / (jnp.sqrt(two * (1.0 / bias_two)) + adam_eps) + decay_rate * old
        master_out[0] = old - learn_rate * update
        one_out[0] = one
        two_out[0] = two

    aliases = {} if before is None else {6: 0, 7: 1, 8: 2}
    extra = () if before is None else before
    return pl.pallas_call(
        body,
        out_shape=(jax.ShapeDtypeStruct(master.shape, jnp.float32),) * 3,
        grid_spec=pltpu.PrefetchScalarGridSpec(
            num_scalar_prefetch=1,
            grid=(kinds, rows // step),
            in_specs=[
                pl.BlockSpec((1, step, half), lambda k, i, s: (k, i, 0)),
                pl.BlockSpec((1, 1, step, half), lambda k, i, s: (s[0], k, i, 0)),
                state,
                state,
                state,
            ]
            + [pl.BlockSpec(memory_space=pl.ANY)] * len(extra),
            out_specs=(state, state, state),
        ),
        input_output_aliases=aliases,
        cost_estimate=pl.CostEstimate(
            flops=20 * kinds * rows * half, bytes_accessed=28 * kinds * rows * half, transcendentals=0
        ),
        name="adam",
    )(place, arrived, partial, master, moment_one, moment_two, *extra)


def grouped(*args):
    return grouped_step(*args)


def grouped_step(tokens, cotangent, working, degraded, block_map, master, moment_one, moment_two):
    replicas = lax.axis_size("dp")
    tp_size = lax.axis_size("tp")
    inner = 2 * CORES
    depth = replicas // inner
    me = lax.axis_index("tp")
    mine = lax.axis_index("dp")
    z, x, core = mine // inner, (mine // CORES) % 2, mine % CORES
    slot_count = working.shape[3] // BLOCK
    per_dev = BLOCKS // tp_size
    half = tokens.shape[1]

    tp_swap = [(i, (i + 1) % tp_size) for i in range(tp_size)]
    x_swap = [(i, i ^ CORES) for i in range(replicas)]
    core_swap = [(i, i ^ 1) for i in range(replicas)]
    after = lax.optimization_barrier

    def over_y(v):
        return lax.ppermute(v, "tp", tp_swap)

    def over_x(v):
        return lax.ppermute(v, "dp", x_swap)

    def over_core(v):
        return lax.ppermute(v, "dp", core_swap)

    def ring(v, step):
        return lax.ppermute(v, "dp", [(i, (i + step * inner) % replicas) for i in range(replicas)])

    order = jnp.arange(BLOCKS, dtype=jnp.int32)
    along = order % depth
    far_x = 1 - (order // depth) % 2
    far_y = 1 - order // per_dev
    block = ((me + far_y) % tp_size) * per_dev + along * 2 + (x ^ far_x)
    places = layout_places(degraded[0], block_map[0], tp_size, slot_count)
    blocks = jnp.arange(BLOCKS, dtype=jnp.int32)
    place = jnp.sum(jnp.where(block[:, None] == blocks[None, :], places[None, :], 0), axis=1)
    held = place // slot_count == me
    slots = jnp.where(held, place % slot_count, 0)
    extra = jnp.where(blocks == 0, me, jnp.where(blocks == 1, core, 0))
    scalars = jnp.concatenate([slots, held.astype(jnp.int32), extra.astype(jnp.int32)])

    t_own, c_own = tokens, cotangent
    t_other = over_y(t_own)
    c_own_x = over_x(c_own)
    t_own_x = over_x(t_own)
    gate, up, down = own_part(scalars, t_own, c_own, working)
    t_other, c_first = after((t_other, c_own))
    c_other = over_y(c_first)
    c_own_c, t_own_c = over_core(c_own), over_core(t_own)
    act, slope, h_theirs, h_far, h_near = gate_up(scalars, t_other, working, gate, up)
    c_other, h_theirs = after((c_other, h_theirs))
    h_from = over_y(h_theirs)
    c_other_x = over_x(c_other)
    grads, d_theirs, d_far, d_near = down_acts(scalars, c_other, working, down, act, slope)
    h_from, d_theirs = after((h_from, d_theirs))
    d_from = over_y(d_theirs)

    def spread(far, near, came):
        far = far + came[0]
        near_x = over_x(far)
        near = near + came[1]
        return [near, near_x, over_core(near[1]), over_core(near_x[1])]

    hidden_acts = spread(h_far, h_near, h_from)
    c_acts = [
        [c_own, c_own_x, c_own_c, over_core(c_own_x)], [c_other, c_other_x, over_core(c_other), over_core(c_other_x)]
    ]
    hidden_acts[1], t_late = after((hidden_acts[1], t_other))
    t_other_x = over_x(t_late)
    t_acts = [
        [t_own, t_own_x, t_own_c, over_core(t_own_x)], [t_other, t_other_x, over_core(t_other), over_core(t_other_x)]
    ]

    parts = [(2, h, weight_grad(hidden_acts, c_acts[h])) for h in range(2)]
    grad_acts = spread(d_far, d_near, d_from)
    parts += [(0, h, weight_grad(grad_acts, t_acts[h])) for h in range(2)]
    steps = (1, -1)
    moving = [None] * len(parts)
    for low in (0, 2):
        for s in range(1, depth):
            for at in (low, low + 1):
                _, h, partial = parts[at]
                chunk = lax.dynamic_index_in_dim(partial, (z - steps[h] * s) % depth, 0, keepdims=False)
                chunk = chunk if moving[at] is None else chunk + moving[at]
                moving[at] = ring(chunk, steps[h])

    sent = over_y(input_part(scalars, grads, working, half, 1))
    kept = input_part(scalars, grads, working, half, 0)
    input_grad = (kept + sent.astype(jnp.float32)).astype(jnp.bfloat16)

    state = None
    for (first, h, partial), arrived in zip(parts, moving):
        where = jnp.stack([z, (me + h) % tp_size]).astype(jnp.int32)
        state = adam(where, arrived, partial, first, master, moment_one, moment_two, state, replicas)
    return (input_grad, *state)


def solution(mesh):
    replicas, tp_size = mesh.shape["dp"], mesh.shape["tp"]
    inner = 2 * CORES

    def per_part(*args):
        half = args[0].shape[1]
        rows = args[5].shape[1]
        aligned = half % BLOCK == 0 and args[0].shape[0] % 16 == 0 and rows * CORES == BLOCK
        split = replicas % (2 * inner) == 0 and tp_size == 2 and BLOCKS == tp_size * replicas // CORES
        return (grouped if aligned and split else per_device)(*args)

    return jax.shard_map(
        per_part,
        mesh=mesh,
        in_specs=(
            P("dp", "tp"),
            P("dp", "tp"),
            P("dp", "tp", None, None, None),
            P("dp"),
            P("dp", None),
            P(None, ("tp", "dp"), None),
            P(None, ("tp", "dp"), None),
            P(None, ("tp", "dp"), None),
        ),
        out_specs=(
            P("dp", "tp"),
            P(None, ("tp", "dp"), None),
            P(None, ("tp", "dp"), None),
            P(None, ("tp", "dp"), None),
        ),
        check_vma=False,
    )
```

```python
import jax
import jax.numpy as jnp
from jax import lax
from jax.experimental import pallas as pl
from jax.experimental.pallas import tpu as pltpu
from jax.sharding import PartitionSpec as P

BLOCK = 128
BLOCKS = 16


beta_one = 0.9
beta_two = 0.95
learn_rate = 0.05
decay_rate = 0.1
adam_eps = 1e-08
bias_one = 1.0 - 0.9**10
bias_two = 1.0 - 0.95**10


def layout_places(replica_flag, mapping, tp_size, slot_count):
    blocks = jnp.arange(BLOCKS, dtype=jnp.int32)
    canonical = blocks // (BLOCKS // tp_size)
    holder = jnp.where(replica_flag > 0, mapping, canonical)
    earlier = (holder[None, :] == holder[:, None]) & (blocks[None, :] < blocks[:, None])
    slot_rank = jnp.sum(earlier.astype(jnp.int32), axis=1)
    return holder * slot_count + slot_rank


def per_device(tokens, cotangent, working, degraded, block_map, master, moment_one, moment_two):
    tp_size = lax.axis_size("tp")
    replicas = lax.axis_size("dp")
    my_index = lax.axis_index("tp")
    weights = working[0, 0]
    slot_count = weights.shape[1] // BLOCK
    per_dev = BLOCKS // tp_size
    places = layout_places(degraded[0], block_map[0], tp_size, slot_count)
    my_slots = my_index * slot_count + jnp.arange(slot_count, dtype=jnp.int32)
    holding = places[:, None] == my_slots[None, :]
    filled = jnp.any(holding, axis=0).astype(jnp.float32)
    column_mask = jnp.repeat(filled, BLOCK)
    inputs, upstream = (
        lax.all_gather(tokens, "tp", axis=1, tiled=True),
        lax.all_gather(cotangent, "tp", axis=1, tiled=True),
    )
    contract_d = (((1,), (1,)), ((), ()))
    gate_pre = lax.dot_general(inputs, weights[0], contract_d, preferred_element_type=jnp.float32)
    up_pre = lax.dot_general(inputs, weights[1], contract_d, preferred_element_type=jnp.float32)
    hidden_grad = lax.dot_general(
        upstream, weights[2], contract_d, preferred_element_type=jnp.float32
    )
    gate_sig = jax.nn.sigmoid(gate_pre)
    active = gate_pre * gate_sig
    hidden = (active * up_pre * column_mask).astype(jnp.bfloat16)
    gate_grad = (
        hidden_grad * up_pre * gate_sig * (1.0 + gate_pre * (1.0 - gate_sig)) * column_mask
    ).astype(jnp.bfloat16)
    up_grad = (hidden_grad * active * column_mask).astype(jnp.bfloat16)
    partial_value = jnp.dot(gate_grad, weights[0], preferred_element_type=jnp.float32) + jnp.dot(
        up_grad, weights[1], preferred_element_type=jnp.float32
    )
    input_grad = lax.psum_scatter(partial_value, "tp", scatter_dimension=1, tiled=True).astype(
        jnp.bfloat16
    )
    tok_rows = gate_grad.shape[0]
    packed = jnp.stack(
        [
            hidden.reshape(tok_rows, slot_count, BLOCK),
            gate_grad.reshape(tok_rows, slot_count, BLOCK),
            up_grad.reshape(tok_rows, slot_count, BLOCK),
        ],
        axis=2,
    )
    packed = packed.transpose(1, 0, 2, 3).reshape(slot_count, tok_rows, 3 * BLOCK)
    selector = holding.astype(jnp.bfloat16)
    outgoing = jnp.einsum(
        "qs,stc->qtc", selector, packed, preferred_element_type=jnp.float32
    ).astype(jnp.bfloat16)
    incoming = lax.all_to_all(outgoing, "tp", split_axis=0, concat_axis=0, tiled=True)
    owned_acts = jnp.sum(incoming.reshape(tp_size, per_dev, tok_rows, 3 * BLOCK), axis=0)
    owned_kinds = (
        owned_acts.reshape(per_dev, tok_rows, 3, BLOCK)
        .transpose(2, 1, 0, 3)
        .reshape(3, tok_rows, per_dev * BLOCK)
    )
    contract_t = (((0,), (0,)), ((), ()))
    gate_term = lax.dot_general(
        owned_kinds[1], inputs, contract_t, preferred_element_type=jnp.float32
    )
    up_term = lax.dot_general(
        owned_kinds[2], inputs, contract_t, preferred_element_type=jnp.float32
    )
    down_term = lax.dot_general(
        owned_kinds[0], upstream, contract_t, preferred_element_type=jnp.float32
    )
    summed = lax.psum_scatter(
        jnp.stack([gate_term, up_term, down_term], axis=1).astype(jnp.bfloat16),
        "dp",
        scatter_dimension=0,
        tiled=True,
    ).astype(jnp.float32)
    grad_mean = jnp.transpose(summed, (1, 0, 2)) / replicas
    moment_one_next = beta_one * moment_one + (1.0 - beta_one) * grad_mean
    moment_two_next = beta_two * moment_two + (1.0 - beta_two) * grad_mean * grad_mean
    update = (
        moment_one_next / bias_one / (jnp.sqrt(moment_two_next / bias_two) + adam_eps)
        + decay_rate * master
    )
    master_next = master - learn_rate * update
    return (input_grad, master_next, moment_one_next, moment_two_next)


CORES = 2
PAIR = 2
contract_last = (((1,), (1,)), ((), ()))
contract_mid = (((1,), (0,)), ((), ()))


def dot32(a, b, dims):
    return lax.dot_general(a, b, dims, preferred_element_type=jnp.float32)


def weight_specs(kinds, half, sides):
    specs = []
    for kind in kinds:
        for side in sides:
            for j in range(PAIR):

                def where(i, s, kind=kind, side=side, j=j):
                    column = s[2 * s.shape[0] // 3] if side == 0 else 1 - s[2 * s.shape[0] // 3]
                    return (0, 0, kind, s[PAIR * i + j], column)

                specs.append(pl.BlockSpec((1, 1, 1, BLOCK, half), where))
    return specs


def whole_spec(shape):
    return pl.BlockSpec(shape, lambda *_: (0,) * len(shape))


def both(first, second):
    return jnp.concatenate([first[0, 0, 0], second[0, 0, 0]], axis=0)


def own_part(scalars, tokens, cotangent, working):
    pairs = scalars.shape[0] // 6
    rows, half = tokens.shape

    def body(s, t_ref, c_ref, *refs):
        weights, outs = refs[:6], refs[6:]
        i = pl.program_id(0)

        @pl.when(s[2 * pairs + 2 * i] + s[2 * pairs + 2 * i + 1] > 0)
        def _():
            for kind, out in enumerate(outs):
                left = c_ref if kind == 2 else t_ref
                out[0] = dot32(left[...], both(*weights[2 * kind : 2 * kind + 2]), contract_last)

    out = jax.ShapeDtypeStruct((pairs, rows, PAIR * BLOCK), jnp.float32)
    return pl.pallas_call(
        body,
        out_shape=(out,) * 3,
        grid_spec=pltpu.PrefetchScalarGridSpec(
            num_scalar_prefetch=1,
            grid=(pairs,),
            in_specs=[whole_spec(tokens.shape)] * 2 + weight_specs((0, 1, 2), half, (0,)),
            out_specs=(pair_spec(rows),) * 3,
        ),
        cost_estimate=pl.CostEstimate(
            flops=6 * rows * half * pairs * PAIR * BLOCK,
            bytes_accessed=6 * half * pairs * PAIR * BLOCK,
            transcendentals=0,
        ),
        name="own_part",
    )(scalars, tokens, cotangent, *[working] * 6)


def pair_spec(rows):
    return pl.BlockSpec((1, rows, PAIR * BLOCK), lambda i, s: (i, 0, 0))


def act_outputs(pairs, kinds, rows):
    quarter = pairs // 4
    part = (quarter, kinds, rows, BLOCK)

    def theirs_at(i, s):
        at = jnp.minimum(i, 2 * quarter - 1)
        return (at // quarter, 0, at % quarter, 0, 0, 0)

    shapes = (
        jax.ShapeDtypeStruct((2, CORES, *part), jnp.bfloat16),
        jax.ShapeDtypeStruct((CORES, *part), jnp.bfloat16),
        jax.ShapeDtypeStruct((CORES, *part), jnp.bfloat16),
    )
    specs = (
        pl.BlockSpec((1, CORES, 1, kinds, rows, BLOCK), theirs_at),
        pl.BlockSpec(
            (CORES, 1, kinds, rows, BLOCK), lambda i, s: (0, jnp.clip(i - 2 * quarter, 0, quarter - 1), 0, 0, 0)
        ),
        pl.BlockSpec(
            (CORES, 1, kinds, rows, BLOCK), lambda i, s: (0, jnp.clip(i - 3 * quarter, 0, quarter - 1), 0, 0, 0)
        ),
    )
    return shapes, specs


def put_acts(i, pairs, core, values, theirs, far, near):
    quarter = pairs // 4
    narrow = BLOCK // CORES
    pieces = [
        [
            jnp.concatenate(
                [value[:, j * BLOCK + c * narrow : j * BLOCK + (c + 1) * narrow] for j in range(PAIR)], axis=1
            ).astype(jnp.bfloat16)
            for c in range(CORES)
        ]
        for value in values
    ]
    slots = [jnp.bitwise_xor(core, c) for c in range(CORES)]

    @pl.when(i < 2 * quarter)
    def _():
        for kind, piece in enumerate(pieces):
            for c in range(CORES):
                theirs[0, slots[c], 0, kind] = piece[c]

    for ref, low in ((far, 2 * quarter), (near, 3 * quarter)):

        @pl.when((i >= low) & (i < low + quarter))
        def _(ref=ref):
            for kind, piece in enumerate(pieces):
                for c in range(CORES):
                    ref[slots[c], 0, kind] = piece[c]


def gate_up(scalars, other, working, gate, up):
    pairs = scalars.shape[0] // 6
    rows, half = other.shape

    def body(s, other_ref, w0, w1, w2, w3, gate_ref, up_ref, act_ref, slope_ref, *outs):
        i = pl.program_id(0)
        has = [s[2 * pairs + 2 * i + j] for j in range(PAIR)]
        core = s[4 * pairs + 1]

        @pl.when(has[0] + has[1] > 0)
        def _():
            zg = gate_ref[0] + dot32(other_ref[...], both(w0, w1), contract_last)
            zu = up_ref[0] + dot32(other_ref[...], both(w2, w3), contract_last)
            lane = lax.broadcasted_iota(jnp.int32, zg.shape, 1)
            keep = jnp.where(lane < BLOCK, has[0], has[1]) > 0
            sig = jax.nn.sigmoid(zg)
            act = zg * sig
            act_ref[0] = act
            slope_ref[0] = zu * sig * (1.0 + zg * (1.0 - sig))
            put_acts(i, pairs, core, [jnp.where(keep, act * zu, 0.0)], *outs)

        @pl.when(has[0] + has[1] == 0)
        def _():
            put_acts(i, pairs, core, [jnp.zeros((rows, PAIR * BLOCK), jnp.float32)], *outs)

    out = jax.ShapeDtypeStruct((pairs, rows, PAIR * BLOCK), jnp.float32)
    shapes, specs = act_outputs(pairs, 1, rows)
    return pl.pallas_call(
        body,
        out_shape=(out, out, *shapes),
        grid_spec=pltpu.PrefetchScalarGridSpec(
            num_scalar_prefetch=1,
            grid=(pairs,),
            in_specs=[whole_spec(other.shape)] + weight_specs((0, 1), half, (1,)) + [pair_spec(rows)] * 2,
            out_specs=(pair_spec(rows), pair_spec(rows), *specs),
        ),
        cost_estimate=pl.CostEstimate(
            flops=4 * rows * half * pairs * PAIR * BLOCK,
            bytes_accessed=4 * half * pairs * PAIR * BLOCK + 16 * rows * pairs * PAIR * BLOCK,
            transcendentals=rows * pairs * PAIR * BLOCK,
        ),
        name="gate_up",
    )(scalars, other, *[working] * 4, gate, up)


def down_acts(scalars, other, working, partial, act, slope):
    pairs = scalars.shape[0] // 6
    rows, half = other.shape

    def body(s, other_ref, w0, w1, partial_ref, act_ref, slope_ref, grads, *outs):
        i = pl.program_id(0)
        has = [s[2 * pairs + 2 * i + j] for j in range(PAIR)]
        core = s[4 * pairs + 1]

        @pl.when(has[0] + has[1] > 0)
        def _():
            dh = partial_ref[0] + dot32(other_ref[...], both(w0, w1), contract_last)
            lane = lax.broadcasted_iota(jnp.int32, dh.shape, 1)
            keep = jnp.where(lane < BLOCK, has[0], has[1]) > 0
            dgate = jnp.where(keep, dh * slope_ref[0], 0.0)
            dup = jnp.where(keep, dh * act_ref[0], 0.0)
            grads[0, 0] = dgate.astype(jnp.bfloat16)
            grads[0, 1] = dup.astype(jnp.bfloat16)
            put_acts(i, pairs, core, [dgate, dup], *outs)

        @pl.when(has[0] + has[1] == 0)
        def _():
            zero = jnp.zeros((rows, PAIR * BLOCK), jnp.float32)
            grads[...] = jnp.zeros(grads.shape, grads.dtype)
            put_acts(i, pairs, core, [zero, zero], *outs)

    shapes, specs = act_outputs(pairs, 2, rows)
    return pl.pallas_call(
        body,
        out_shape=(jax.ShapeDtypeStruct((pairs, 2, rows, PAIR * BLOCK), jnp.bfloat16), *shapes),
        grid_spec=pltpu.PrefetchScalarGridSpec(
            num_scalar_prefetch=1,
            grid=(pairs,),
            in_specs=[whole_spec(other.shape)] + weight_specs((2,), half, (1,)) + [pair_spec(rows)] * 3,
            out_specs=(pl.BlockSpec((1, 2, rows, PAIR * BLOCK), lambda i, s: (i, 0, 0, 0)), *specs),
        ),
        cost_estimate=pl.CostEstimate(
            flops=2 * rows * half * pairs * PAIR * BLOCK,
            bytes_accessed=2 * half * pairs * PAIR * BLOCK + 20 * rows * pairs * PAIR * BLOCK,
            transcendentals=0,
        ),
        name="down_acts",
    )(scalars, other, *[working] * 2, partial, act, slope)


def input_part(scalars, grads, working, half, side):
    pairs = scalars.shape[0] // 6
    rows = grads.shape[2]

    def body(s, grads_ref, w0, w1, w2, w3, out_ref, total):
        i = pl.program_id(0)

        @pl.when(i == 0)
        def _():
            total[...] = jnp.zeros(total.shape, total.dtype)

        @pl.when(s[2 * pairs + 2 * i] + s[2 * pairs + 2 * i + 1] > 0)
        def _():
            total[...] += dot32(grads_ref[0, 0], both(w0, w1), contract_mid) + dot32(
                grads_ref[0, 1], both(w2, w3), contract_mid
            )

        @pl.when(i == pairs - 1)
        def _():
            out_ref[...] = total[...].astype(out_ref.dtype)

    return pl.pallas_call(
        body,
        out_shape=jax.ShapeDtypeStruct((rows, half), jnp.bfloat16 if side else jnp.float32),
        grid_spec=pltpu.PrefetchScalarGridSpec(
            num_scalar_prefetch=1,
            grid=(pairs,),
            in_specs=[pl.BlockSpec((1, 2, rows, PAIR * BLOCK), lambda i, s: (i, 0, 0, 0))]
            + weight_specs((0, 1), half, (side,)),
            out_specs=whole_spec((rows, half)),
            scratch_shapes=[pltpu.VMEM((rows, half), jnp.float32)],
        ),
        cost_estimate=pl.CostEstimate(
            flops=4 * rows * half * pairs * PAIR * BLOCK,
            bytes_accessed=4 * half * pairs * PAIR * BLOCK,
            transcendentals=0,
        ),
        name="input_other" if side else "input_own",
    )(scalars, grads, *[working] * 4)


def weight_grad(acts, inputs, kind, own):
    group = len(acts)
    quarter, _, rows, _ = acts[0].shape[-4:]
    half = inputs[0].shape[1]
    narrow = BLOCK // CORES
    wide = quarter * BLOCK
    owners = PAIR * quarter
    tile = half // 2 if half % (2 * BLOCK) == 0 else half

    def body(s, *refs):
        a_refs, x_refs, outs = refs[:group], refs[group : 2 * group], refs[2 * group : 2 * group + owners]
        left, value = refs[2 * group + owners :]

        @pl.when(pl.program_id(0) == 0)
        def _():
            for p in range(quarter):
                column = jnp.concatenate(
                    [ref[0, p, 0] if len(ref.shape) == 5 else ref[p, 0] for ref in a_refs], axis=0
                )
                left[p * BLOCK : (p + 1) * BLOCK, :] = column.T

        right = jnp.concatenate([ref[...] for ref in x_refs], axis=0)
        value[...] = dot32(left[...], right, contract_mid).astype(jnp.bfloat16)
        for relation, out_ref in enumerate(outs):
            start = pl.multiple_of(jnp.bitwise_xor(s[0], relation) * narrow, narrow)
            out_ref[...] = value[pl.ds(start, narrow), :]

    def act_spec(a):
        if a.ndim == 5:
            return pl.BlockSpec((1, quarter, 1, rows, BLOCK), lambda i, s: (0, 0, kind, 0, 0))
        return pl.BlockSpec((quarter, 1, rows, BLOCK), lambda i, s: (0, kind, 0, 0))

    out = jax.ShapeDtypeStruct((narrow, half), jnp.bfloat16)
    return pl.pallas_call(
        body,
        out_shape=(out,) * owners,
        grid_spec=pltpu.PrefetchScalarGridSpec(
            num_scalar_prefetch=1,
            grid=(half // tile,),
            in_specs=[act_spec(a) for a in acts] + [pl.BlockSpec((rows, tile), lambda i, s: (0, i))] * group,
            out_specs=(pl.BlockSpec((narrow, tile), lambda i, s: (0, i)),) * owners,
            scratch_shapes=[
                pltpu.VMEM((wide, group * rows), jnp.bfloat16),
                pltpu.VMEM((wide, tile), jnp.bfloat16),
            ],
        ),
        cost_estimate=pl.CostEstimate(
            flops=2 * group * rows * wide * half,
            bytes_accessed=2 * group * rows * half + 2 * wide * half,
            transcendentals=0,
        ),
    )(own, *acts, *inputs)


def adam(me, sums, kinds, halves, master, moment_one, moment_two, before, replicas):
    rows, half = sums[0][0].shape
    count = len(sums[0])
    steps = len(sums)
    columns = master.shape[2] // half

    def at(i, s):
        kind = kinds[0] + i * (kinds[1] - kinds[0])
        return (kind, 0, (s[0] + halves[0] + i * (halves[1] - halves[0])) % columns)

    state = pl.BlockSpec((1, rows, half), at)

    def body(s, *refs):
        parts, (master_ref, one_ref, two_ref) = refs[: steps * count], refs[steps * count : steps * count + 3]
        master_out, one_out, two_out = refs[-3:]
        for i in range(steps):

            @pl.when(pl.program_id(0) == i)
            def _(i=i):
                summed = parts[i * count][...].astype(jnp.float32)
                for part in parts[i * count + 1 : (i + 1) * count]:
                    summed = summed + part[...].astype(jnp.float32)
                grad_mean = summed * (1.0 / replicas)
                one = beta_one * one_ref[0] + (1.0 - beta_one) * grad_mean
                two = beta_two * two_ref[0] + (1.0 - beta_two) * grad_mean * grad_mean
                old = master_ref[0]
                update = one * (1.0 / bias_one) / (jnp.sqrt(two * (1.0 / bias_two)) + adam_eps) + decay_rate * old
                master_out[0] = old - learn_rate * update
                one_out[0] = one
                two_out[0] = two

    extra = () if before is None else before
    flat = [part for group in sums for part in group]
    return pl.pallas_call(
        body,
        out_shape=(jax.ShapeDtypeStruct(master.shape, jnp.float32),) * 3,
        grid_spec=pltpu.PrefetchScalarGridSpec(
            num_scalar_prefetch=1,
            grid=(steps,),
            in_specs=[pl.BlockSpec((rows, half), lambda i, s: (0, 0))] * len(flat)
            + [state] * 3
            + [pl.BlockSpec(memory_space=pl.ANY)] * len(extra),
            out_specs=(state,) * 3,
        ),
        input_output_aliases={len(flat) + 4 + i: i for i in range(len(extra))},
        cost_estimate=pl.CostEstimate(
            flops=20 * steps * rows * half, bytes_accessed=28 * steps * rows * half, transcendentals=0
        ),
        name="adam",
    )(me, *flat, master, moment_one, moment_two, *extra)


def grouped(*args):
    return grouped_step(*args)


def grouped_step(tokens, cotangent, working, degraded, block_map, master, moment_one, moment_two):
    replicas = lax.axis_size("dp")
    tp_size = lax.axis_size("tp")
    me = lax.axis_index("tp")
    mine = lax.axis_index("dp")
    core, x = mine % CORES, (mine // CORES) % 2
    zs, zp = (mine // (2 * CORES)) % 2, mine // (4 * CORES)
    slot_count = working.shape[3] // BLOCK
    per_dev = BLOCKS // tp_size
    half = tokens.shape[1]
    after = lax.optimization_barrier

    def over_y(v):
        return lax.ppermute(v, "tp", [(i, (i + 1) % tp_size) for i in range(tp_size)])

    def over(bit, v):
        pairs = [(i, i ^ bit) for i in range(replicas)]
        return lax.ppermute(v, "dp", pairs)

    def over_core(v):
        return over(1, v)

    def over_x(v):
        return over(CORES, v)

    def over_s(v):
        return over(2 * CORES, v)

    def over_m(v):
        return over(4 * CORES, v)

    order = jnp.arange(BLOCKS, dtype=jnp.int32)
    far_y, far_s = 1 - order // per_dev, 1 - (order // 4) % 2
    block = ((me + far_y) % tp_size) * per_dev + ((order // 2) % 2) * 4 + (zs ^ far_s) * 2 + order % 2
    places = layout_places(degraded[0], block_map[0], tp_size, slot_count)
    blocks = jnp.arange(BLOCKS, dtype=jnp.int32)
    place = jnp.sum(jnp.where(block[:, None] == blocks[None, :], places[None, :], 0), axis=1)
    held = place // slot_count == me
    slots = jnp.where(held, place % slot_count, 0)
    extra = jnp.where(blocks == 0, me, jnp.where(blocks == 1, core, 0))
    scalars = jnp.concatenate([slots, held.astype(jnp.int32), extra.astype(jnp.int32)])
    own = (zp * 2 + x).astype(jnp.int32).reshape(1)

    t_own, c_own = tokens, cotangent
    t_other = over_y(t_own)
    c_own_s = over_s(c_own)
    t_own_s = over_s(t_own)
    gate, up, down = own_part(scalars, t_own, c_own, working)
    t_other, c_first = after((t_other, c_own))
    c_other = over_y(c_first)
    c_own_c, t_own_c = over_core(c_own), over_core(t_own)
    act, slope, h_theirs, h_far, h_near = gate_up(scalars, t_other, working, gate, up)
    c_other, h_theirs = after((c_other, h_theirs))
    h_from = over_y(h_theirs)
    c_other_s = over_s(c_other)
    grads, d_theirs, d_far, d_near = down_acts(scalars, c_other, working, down, act, slope)
    h_from, d_theirs = after((h_from, d_theirs))
    d_from = over_y(d_theirs)

    def spread(far, near, came):
        far = far + came[0]
        near_s = over_s(far)
        near = near + came[1]
        return [near, near_s, over_core(near[1]), over_core(near_s[1])]

    hidden_acts = spread(h_far, h_near, h_from)
    c_acts = [
        [c_own, c_own_s, c_own_c, over_core(c_own_s)], [c_other, c_other_s, over_core(c_other), over_core(c_other_s)]
    ]
    hidden_acts[1], t_late = after((hidden_acts[1], t_other))
    t_other_s = over_s(t_late)
    t_acts = [
        [t_own, t_own_s, t_own_c, over_core(t_own_s)], [t_other, t_other_s, over_core(t_other), over_core(t_other_s)]
    ]
    grad_acts = spread(d_far, d_near, d_from)

    sums = []
    for kind, h in PIECES:
        acts, inputs = (hidden_acts, c_acts[h]) if kind == 2 else (grad_acts, t_acts[h])
        keep, far_x, far_z, far_both = weight_grad(acts, inputs, kind % 2, own)
        came = over_x(far_both)
        far_z = far_z + came
        sums.append((keep, over_x(far_x), over_m(far_z)))
    state = None
    for at in range(0, len(PIECES), 2):
        kinds, halves = zip(*PIECES[at : at + 2])
        state = adam(
            me.astype(jnp.int32).reshape(1),
            sums[at : at + 2],
            kinds,
            halves,
            master,
            moment_one,
            moment_two,
            state,
            replicas,
        )

    sent = over_y(input_part(scalars, grads, working, half, 1))
    kept = input_part(scalars, grads, working, half, 0)
    input_grad = (kept + sent.astype(jnp.float32)).astype(jnp.bfloat16)
    return (input_grad, *state)


PIECES = ((2, 0), (2, 1), (0, 0), (1, 0), (0, 1), (1, 1))


def solution(mesh):
    replicas, tp_size = mesh.shape["dp"], mesh.shape["tp"]

    def per_part(*args):
        half = args[0].shape[1]
        rows = args[5].shape[1]
        aligned = half % BLOCK == 0 and args[0].shape[0] % 16 == 0 and rows * CORES == BLOCK
        split = replicas == 8 * CORES and tp_size == 2 and BLOCKS == tp_size * replicas // CORES
        return (grouped if aligned and split else per_device)(*args)

    return jax.shard_map(
        per_part,
        mesh=mesh,
        in_specs=(
            P("dp", "tp"),
            P("dp", "tp"),
            P("dp", "tp", None, None, None),
            P("dp"),
            P("dp", None),
            P(None, ("tp", "dp"), None),
            P(None, ("tp", "dp"), None),
            P(None, ("tp", "dp"), None),
        ),
        out_specs=(
            P("dp", "tp"),
            P(None, ("tp", "dp"), None),
            P(None, ("tp", "dp"), None),
            P(None, ("tp", "dp"), None),
        ),
        check_vma=False,
    )
```

```python
import jax
import jax.numpy as jnp
from jax import lax
from jax.experimental import pallas as pl
from jax.experimental.pallas import tpu as pltpu
from jax.sharding import PartitionSpec as P

BLOCK = 128
BLOCKS = 16


beta_one = 0.9
beta_two = 0.95
learn_rate = 0.05
decay_rate = 0.1
adam_eps = 1e-08
bias_one = 1.0 - 0.9**10
bias_two = 1.0 - 0.95**10


def layout_places(replica_flag, mapping, tp_size, slot_count):
    blocks = jnp.arange(BLOCKS, dtype=jnp.int32)
    canonical = blocks // (BLOCKS // tp_size)
    holder = jnp.where(replica_flag > 0, mapping, canonical)
    earlier = (holder[None, :] == holder[:, None]) & (blocks[None, :] < blocks[:, None])
    slot_rank = jnp.sum(earlier.astype(jnp.int32), axis=1)
    return holder * slot_count + slot_rank


def per_device(tokens, cotangent, working, degraded, block_map, master, moment_one, moment_two):
    tp_size = lax.axis_size("tp")
    replicas = lax.axis_size("dp")
    my_index = lax.axis_index("tp")
    weights = working[0, 0]
    slot_count = weights.shape[1] // BLOCK
    per_dev = BLOCKS // tp_size
    places = layout_places(degraded[0], block_map[0], tp_size, slot_count)
    my_slots = my_index * slot_count + jnp.arange(slot_count, dtype=jnp.int32)
    holding = places[:, None] == my_slots[None, :]
    filled = jnp.any(holding, axis=0).astype(jnp.float32)
    column_mask = jnp.repeat(filled, BLOCK)
    inputs, upstream = (
        lax.all_gather(tokens, "tp", axis=1, tiled=True),
        lax.all_gather(cotangent, "tp", axis=1, tiled=True),
    )
    contract_d = (((1,), (1,)), ((), ()))
    gate_pre = lax.dot_general(inputs, weights[0], contract_d, preferred_element_type=jnp.float32)
    up_pre = lax.dot_general(inputs, weights[1], contract_d, preferred_element_type=jnp.float32)
    hidden_grad = lax.dot_general(
        upstream, weights[2], contract_d, preferred_element_type=jnp.float32
    )
    gate_sig = jax.nn.sigmoid(gate_pre)
    active = gate_pre * gate_sig
    hidden = (active * up_pre * column_mask).astype(jnp.bfloat16)
    gate_grad = (
        hidden_grad * up_pre * gate_sig * (1.0 + gate_pre * (1.0 - gate_sig)) * column_mask
    ).astype(jnp.bfloat16)
    up_grad = (hidden_grad * active * column_mask).astype(jnp.bfloat16)
    partial_value = jnp.dot(gate_grad, weights[0], preferred_element_type=jnp.float32) + jnp.dot(
        up_grad, weights[1], preferred_element_type=jnp.float32
    )
    input_grad = lax.psum_scatter(partial_value, "tp", scatter_dimension=1, tiled=True).astype(
        jnp.bfloat16
    )
    tok_rows = gate_grad.shape[0]
    packed = jnp.stack(
        [
            hidden.reshape(tok_rows, slot_count, BLOCK),
            gate_grad.reshape(tok_rows, slot_count, BLOCK),
            up_grad.reshape(tok_rows, slot_count, BLOCK),
        ],
        axis=2,
    )
    packed = packed.transpose(1, 0, 2, 3).reshape(slot_count, tok_rows, 3 * BLOCK)
    selector = holding.astype(jnp.bfloat16)
    outgoing = jnp.einsum(
        "qs,stc->qtc", selector, packed, preferred_element_type=jnp.float32
    ).astype(jnp.bfloat16)
    incoming = lax.all_to_all(outgoing, "tp", split_axis=0, concat_axis=0, tiled=True)
    owned_acts = jnp.sum(incoming.reshape(tp_size, per_dev, tok_rows, 3 * BLOCK), axis=0)
    owned_kinds = (
        owned_acts.reshape(per_dev, tok_rows, 3, BLOCK)
        .transpose(2, 1, 0, 3)
        .reshape(3, tok_rows, per_dev * BLOCK)
    )
    contract_t = (((0,), (0,)), ((), ()))
    gate_term = lax.dot_general(
        owned_kinds[1], inputs, contract_t, preferred_element_type=jnp.float32
    )
    up_term = lax.dot_general(
        owned_kinds[2], inputs, contract_t, preferred_element_type=jnp.float32
    )
    down_term = lax.dot_general(
        owned_kinds[0], upstream, contract_t, preferred_element_type=jnp.float32
    )
    summed = lax.psum_scatter(
        jnp.stack([gate_term, up_term, down_term], axis=1).astype(jnp.bfloat16),
        "dp",
        scatter_dimension=0,
        tiled=True,
    ).astype(jnp.float32)
    grad_mean = jnp.transpose(summed, (1, 0, 2)) / replicas
    moment_one_next = beta_one * moment_one + (1.0 - beta_one) * grad_mean
    moment_two_next = beta_two * moment_two + (1.0 - beta_two) * grad_mean * grad_mean
    update = (
        moment_one_next / bias_one / (jnp.sqrt(moment_two_next / bias_two) + adam_eps)
        + decay_rate * master
    )
    master_next = master - learn_rate * update
    return (input_grad, master_next, moment_one_next, moment_two_next)


CORES = 2
WIDE = 4 * BLOCK
contract_last = (((1,), (1,)), ((), ()))
contract_mid = (((1,), (0,)), ((), ()))


def dot32(a, b, dims):
    return lax.dot_general(a, b, dims, preferred_element_type=jnp.float32)


FLAG, HOLDER, ME, CORE, NEAR = range(5)


def group_of(i, s, tp_size, depth):
    owner = (s[ME] + 1 + i // depth) % tp_size
    held = jnp.where(s[FLAG] > 0, s[HOLDER] == s[ME], owner == s[ME])
    place = jnp.where(s[FLAG] > 0, owner * depth + i % depth, i % depth)
    return held, jnp.where(held, place, 0)


def weight_specs(kinds, half, sides, layout):
    def spec(kind, side):
        def where(i, s):
            _, place = group_of(i, s, *layout)
            return (0, 0, kind, place, s[ME] if side == 0 else 1 - s[ME])

        return pl.BlockSpec((1, 1, 1, WIDE, half), where)

    return [spec(kind, side) for kind in kinds for side in sides]


def whole_spec(shape):
    return pl.BlockSpec(shape, lambda *_: (0,) * len(shape))


def step_spec(rows):
    return pl.BlockSpec((1, rows, WIDE), lambda i, s: (i, 0, 0))


def own_part(scalars, tokens, cotangent, working, layout):
    steps = layout[0] * layout[1]
    rows, half = tokens.shape

    def body(s, t_ref, c_ref, *refs):
        weights, outs = refs[:3], refs[3:]
        held, _ = group_of(pl.program_id(0), s, *layout)

        @pl.when(held)
        def _():
            for kind, out in enumerate(outs):
                left = c_ref if kind == 2 else t_ref
                out[0] = dot32(left[...], weights[kind][0, 0, 0], contract_last)

    out = jax.ShapeDtypeStruct((steps, rows, WIDE), jnp.float32)
    return pl.pallas_call(
        body,
        out_shape=(out,) * 3,
        grid_spec=pltpu.PrefetchScalarGridSpec(
            num_scalar_prefetch=1,
            grid=(steps,),
            in_specs=[whole_spec(tokens.shape)] * 2 + weight_specs((0, 1, 2), half, (0,), layout),
            out_specs=(step_spec(rows),) * 3,
        ),
        cost_estimate=pl.CostEstimate(
            flops=6 * rows * half * steps * WIDE, bytes_accessed=6 * half * steps * WIDE, transcendentals=0
        ),
        name="own_part",
    )(scalars, tokens, cotangent, *[working] * 3)


def act_outputs(layout, kinds, rows):
    depth = layout[1]
    block = (2, CORES, 1, kinds, rows, BLOCK)
    shape = jax.ShapeDtypeStruct((2, CORES, depth, kinds, rows, BLOCK), jnp.bfloat16)
    specs = (
        pl.BlockSpec(block, lambda i, s: (0, 0, jnp.minimum(i, depth - 1), 0, 0, 0)),
        pl.BlockSpec(block, lambda i, s: (0, 0, jnp.maximum(i - depth, 0), 0, 0, 0)),
    )
    return (shape, shape), specs


def put_acts(i, s, layout, values, theirs, mine):
    narrow = BLOCK // CORES

    def put(ref):
        for kind, value in enumerate(values):
            for side in range(2):
                for c in range(CORES):
                    starts = [(side * 2 + j) * BLOCK + c * narrow for j in range(2)]
                    piece = jnp.concatenate([value[:, at : at + narrow] for at in starts], axis=1)
                    ref[jnp.bitwise_xor(s[NEAR], side), jnp.bitwise_xor(s[CORE], c), 0, kind] = piece.astype(
                        jnp.bfloat16
                    )

    pl.when(i < layout[1])(lambda: put(theirs))
    pl.when(i >= layout[1])(lambda: put(mine))


def clear_acts(i, layout, theirs, mine):
    def clear(ref):
        ref[...] = jnp.zeros(ref.shape, ref.dtype)

    pl.when(i < layout[1])(lambda: clear(theirs))
    pl.when(i >= layout[1])(lambda: clear(mine))


def gate_up(scalars, other, working, gate, up, layout):
    steps = layout[0] * layout[1]
    rows, half = other.shape

    def body(s, other_ref, w0, w1, gate_ref, up_ref, act_ref, slope_ref, *outs):
        i = pl.program_id(0)
        held, _ = group_of(i, s, *layout)

        @pl.when(held)
        def _():
            zg = gate_ref[0] + dot32(other_ref[...], w0[0, 0, 0], contract_last)
            zu = up_ref[0] + dot32(other_ref[...], w1[0, 0, 0], contract_last)
            sig = jax.nn.sigmoid(zg)
            act = zg * sig
            act_ref[0] = act
            slope_ref[0] = zu * sig * (1.0 + zg * (1.0 - sig))
            put_acts(i, s, layout, [act * zu], *outs)

        pl.when(jnp.logical_not(held))(lambda: clear_acts(i, layout, *outs))

    out = jax.ShapeDtypeStruct((steps, rows, WIDE), jnp.float32)
    shapes, specs = act_outputs(layout, 1, rows)
    return pl.pallas_call(
        body,
        out_shape=(out, out, *shapes),
        grid_spec=pltpu.PrefetchScalarGridSpec(
            num_scalar_prefetch=1,
            grid=(steps,),
            in_specs=[whole_spec(other.shape)] + weight_specs((0, 1), half, (1,), layout) + [step_spec(rows)] * 2,
            out_specs=(step_spec(rows), step_spec(rows), *specs),
        ),
        cost_estimate=pl.CostEstimate(
            flops=4 * rows * half * steps * WIDE,
            bytes_accessed=4 * half * steps * WIDE + 16 * rows * steps * WIDE,
            transcendentals=rows * steps * WIDE,
        ),
        name="gate_up",
    )(scalars, other, *[working] * 2, gate, up)


def down_acts(scalars, other, working, partial, act, slope, layout):
    steps = layout[0] * layout[1]
    rows, half = other.shape

    def body(s, other_ref, w0, partial_ref, act_ref, slope_ref, grads, *outs):
        i = pl.program_id(0)
        held, _ = group_of(i, s, *layout)

        @pl.when(held)
        def _():
            dh = partial_ref[0] + dot32(other_ref[...], w0[0, 0, 0], contract_last)
            dgate = dh * slope_ref[0]
            dup = dh * act_ref[0]
            grads[0, 0] = dgate.astype(jnp.bfloat16)
            grads[0, 1] = dup.astype(jnp.bfloat16)
            put_acts(i, s, layout, [dgate, dup], *outs)

        pl.when(jnp.logical_not(held))(lambda: clear_acts(i, layout, *outs))

    shapes, specs = act_outputs(layout, 2, rows)
    return pl.pallas_call(
        body,
        out_shape=(jax.ShapeDtypeStruct((steps, 2, rows, WIDE), jnp.bfloat16), *shapes),
        grid_spec=pltpu.PrefetchScalarGridSpec(
            num_scalar_prefetch=1,
            grid=(steps,),
            in_specs=[whole_spec(other.shape)] + weight_specs((2,), half, (1,), layout) + [step_spec(rows)] * 3,
            out_specs=(pl.BlockSpec((1, 2, rows, WIDE), lambda i, s: (i, 0, 0, 0)), *specs),
        ),
        cost_estimate=pl.CostEstimate(
            flops=2 * rows * half * steps * WIDE,
            bytes_accessed=2 * half * steps * WIDE + 20 * rows * steps * WIDE,
            transcendentals=0,
        ),
        name="down_acts",
    )(scalars, other, working, partial, act, slope)


def input_part(scalars, grads, working, half, side, layout):
    steps = layout[0] * layout[1]
    rows = grads.shape[2]

    def body(s, grads_ref, w0, w1, out_ref, total):
        i = pl.program_id(0)
        held, _ = group_of(i, s, *layout)

        @pl.when(i == 0)
        def _():
            total[...] = jnp.zeros(total.shape, total.dtype)

        @pl.when(held)
        def _():
            total[...] += dot32(grads_ref[0, 0], w0[0, 0, 0], contract_mid) + dot32(
                grads_ref[0, 1], w1[0, 0, 0], contract_mid
            )

        @pl.when(i == steps - 1)
        def _():
            out_ref[...] = total[...].astype(out_ref.dtype)

    return pl.pallas_call(
        body,
        out_shape=jax.ShapeDtypeStruct((rows, half), jnp.bfloat16 if side else jnp.float32),
        grid_spec=pltpu.PrefetchScalarGridSpec(
            num_scalar_prefetch=1,
            grid=(steps,),
            in_specs=[pl.BlockSpec((1, 2, rows, WIDE), lambda i, s: (i, 0, 0, 0))]
            + weight_specs((0, 1), half, (side,), layout),
            out_specs=whole_spec((rows, half)),
            scratch_shapes=[pltpu.VMEM((rows, half), jnp.float32)],
        ),
        cost_estimate=pl.CostEstimate(
            flops=4 * rows * half * steps * WIDE, bytes_accessed=4 * half * steps * WIDE, transcendentals=0
        ),
        name="input_other" if side else "input_own",
    )(scalars, grads, *[working] * 2)


def weight_grad(acts, inputs, own):
    group = len(acts)
    depth, kinds, rows, _ = acts[0].shape[-4:]
    half = inputs[0].shape[1]
    narrow = BLOCK // CORES
    wide = depth * BLOCK
    owners = wide // narrow
    tile = half // 2 if half % (2 * BLOCK) == 0 else half

    def body(s, *refs):
        a_refs, x_refs, outs = refs[:group], refs[group : 2 * group], refs[2 * group : 2 * group + kinds * owners]
        left, value = refs[2 * group + kinds * owners :]

        @pl.when(pl.program_id(0) == 0)
        def _():
            for kind in range(kinds):
                for p in range(depth):
                    column = jnp.concatenate(
                        [ref[0, p, kind] if len(ref.shape) == 5 else ref[p, kind] for ref in a_refs], axis=0
                    )
                    left[kind, p * BLOCK : (p + 1) * BLOCK, :] = column.T

        right = jnp.concatenate([ref[...] for ref in x_refs], axis=0)
        for kind in range(kinds):
            value[...] = dot32(left[kind], right, contract_mid).astype(jnp.bfloat16)
            for relation in range(owners):
                start = pl.multiple_of(jnp.bitwise_xor(s[0], relation) * narrow, narrow)
                outs[kind * owners + relation][...] = value[pl.ds(start, narrow), :]

    def act_spec(a):
        if a.ndim == 5:
            return pl.BlockSpec((1, *a.shape[1:]), lambda i, s: (0,) * 5)
        return pl.BlockSpec(a.shape, lambda i, s: (0,) * 4)

    out = jax.ShapeDtypeStruct((narrow, half), jnp.bfloat16)
    made = pl.pallas_call(
        body,
        out_shape=(out,) * (kinds * owners),
        grid_spec=pltpu.PrefetchScalarGridSpec(
            num_scalar_prefetch=1,
            grid=(half // tile,),
            in_specs=[act_spec(a) for a in acts] + [pl.BlockSpec((rows, tile), lambda i, s: (0, i))] * group,
            out_specs=(pl.BlockSpec((narrow, tile), lambda i, s: (0, i)),) * (kinds * owners),
            scratch_shapes=[
                pltpu.VMEM((kinds, wide, group * rows), jnp.bfloat16),
                pltpu.VMEM((wide, tile), jnp.bfloat16),
            ],
        ),
        cost_estimate=pl.CostEstimate(
            flops=2 * kinds * group * rows * wide * half,
            bytes_accessed=2 * group * rows * half + 2 * kinds * wide * half,
            transcendentals=0,
        ),
    )(own, *acts, *inputs)
    return [made[kind * owners : (kind + 1) * owners] for kind in range(kinds)]


def adam(me, sums, kinds, halves, master, moment_one, moment_two, before, replicas):
    rows, half = sums[0][0].shape
    count = len(sums[0])
    steps = len(sums)
    columns = master.shape[2] // half

    def at(i, s):
        kind = kinds[0] + i * (kinds[1] - kinds[0])
        return (kind, 0, (s[0] + halves[0] + i * (halves[1] - halves[0])) % columns)

    state = pl.BlockSpec((1, rows, half), at)

    def body(s, *refs):
        parts, (master_ref, one_ref, two_ref) = refs[: steps * count], refs[steps * count : steps * count + 3]
        master_out, one_out, two_out = refs[-3:]
        for i in range(steps):

            @pl.when(pl.program_id(0) == i)
            def _(i=i):
                summed = parts[i * count][...].astype(jnp.float32)
                for part in parts[i * count + 1 : (i + 1) * count]:
                    summed = summed + part[...].astype(jnp.float32)
                grad_mean = summed * (1.0 / replicas)
                one = beta_one * one_ref[0] + (1.0 - beta_one) * grad_mean
                two = beta_two * two_ref[0] + (1.0 - beta_two) * grad_mean * grad_mean
                old = master_ref[0]
                update = one * (1.0 / bias_one) / (jnp.sqrt(two * (1.0 / bias_two)) + adam_eps) + decay_rate * old
                master_out[0] = old - learn_rate * update
                one_out[0] = one
                two_out[0] = two

    extra = () if before is None else before
    flat = [part for group in sums for part in group]
    return pl.pallas_call(
        body,
        out_shape=(jax.ShapeDtypeStruct(master.shape, jnp.float32),) * 3,
        grid_spec=pltpu.PrefetchScalarGridSpec(
            num_scalar_prefetch=1,
            grid=(steps,),
            in_specs=[pl.BlockSpec((rows, half), lambda i, s: (0, 0))] * len(flat)
            + [state] * 3
            + [pl.BlockSpec(memory_space=pl.ANY)] * len(extra),
            out_specs=(state,) * 3,
        ),
        input_output_aliases={len(flat) + 4 + i: i for i in range(len(extra))},
        cost_estimate=pl.CostEstimate(
            flops=20 * steps * rows * half, bytes_accessed=28 * steps * rows * half, transcendentals=0
        ),
        name="adam",
    )(me, *flat, master, moment_one, moment_two, *extra)


def grouped(*args):
    return grouped_step(*args)


def grouped_step(tokens, cotangent, working, degraded, block_map, master, moment_one, moment_two):
    replicas = lax.axis_size("dp")
    tp_size = lax.axis_size("tp")
    me = lax.axis_index("tp")
    mine = lax.axis_index("dp")
    core, x = mine % CORES, (mine // CORES) % 2
    zs, zp = (mine // (2 * CORES)) % 2, mine // (4 * CORES)
    per_dev = BLOCKS // tp_size
    half = tokens.shape[1]
    after = lax.optimization_barrier

    def over_y(v):
        return lax.ppermute(v, "tp", [(i, (i + 1) % tp_size) for i in range(tp_size)])

    def over(bit, v):
        pairs = [(i, i ^ bit) for i in range(replicas)]
        return lax.ppermute(v, "dp", pairs)

    def over_core(v):
        return over(1, v)

    def over_x(v):
        return over(CORES, v)

    def over_s(v):
        return over(2 * CORES, v)

    def over_m(v):
        return over(4 * CORES, v)

    layout = (tp_size, per_dev * BLOCK // WIDE)
    scalars = jnp.stack([degraded[0], block_map[0, 0], me, core, zs]).astype(jnp.int32)
    own = (zp * 2 + x).astype(jnp.int32).reshape(1)

    t_own, c_own = tokens, cotangent
    t_other = over_y(t_own)
    c_own_s = over_s(c_own)
    t_own_s = over_s(t_own)
    gate, up, down = own_part(scalars, t_own, c_own, working, layout)
    t_other, c_first = after((t_other, c_own))
    c_other = over_y(c_first)
    c_own_c, t_own_c = over_core(c_own), over_core(t_own)
    act, slope, h_theirs, h_mine = gate_up(scalars, t_other, working, gate, up, layout)
    c_other, h_theirs = after((c_other, h_theirs))
    h_from = over_y(h_theirs)
    c_other_s = over_s(c_other)
    grads, d_theirs, d_mine = down_acts(scalars, c_other, working, down, act, slope, layout)
    h_from, d_theirs = after((h_from, d_theirs))
    d_from = over_y(d_theirs)

    def spread(mine, came):
        far = mine[1] + came[1]
        near_s = over_s(far)
        near = mine[0] + came[0]
        return [near, near_s, over_core(near[1]), over_core(near_s[1])]

    hidden_acts = spread(h_mine, h_from)
    t_other_s = over_s(t_other)
    c_acts = [
        [c_own, c_own_s, c_own_c, over_core(c_own_s)], [c_other, c_other_s, over_core(c_other), over_core(c_other_s)]
    ]
    t_acts = [
        [t_own, t_own_s, t_own_c, over_core(t_own_s)], [t_other, t_other_s, over_core(t_other), over_core(t_other_s)]
    ]
    grad_acts = spread(d_mine, d_from)

    made = []
    for h in range(2):
        made += weight_grad(hidden_acts, c_acts[h], own)
    for h in range(2):
        made += weight_grad(grad_acts, t_acts[h], own)
    sums = []
    for keep, far_x, far_z, far_both in made:
        came = over_x(far_both)
        far_z = (far_z.astype(jnp.float32) + came.astype(jnp.float32)).astype(jnp.bfloat16)
        sums.append((keep, over_x(far_x), over_m(far_z)))
    state = None
    for at in range(0, len(PIECES), 2):
        kinds, halves = zip(*PIECES[at : at + 2])
        state = adam(
            me.astype(jnp.int32).reshape(1),
            sums[at : at + 2],
            kinds,
            halves,
            master,
            moment_one,
            moment_two,
            state,
            replicas,
        )

    sent = over_y(input_part(scalars, grads, working, half, 1, layout))
    kept = input_part(scalars, grads, working, half, 0, layout)
    input_grad = (kept + sent.astype(jnp.float32)).astype(jnp.bfloat16)
    return (input_grad, *state)


PIECES = ((2, 0), (2, 1), (0, 0), (1, 0), (0, 1), (1, 1))


def solution(mesh):
    replicas, tp_size = mesh.shape["dp"], mesh.shape["tp"]

    def per_part(*args):
        half = args[0].shape[1]
        rows = args[5].shape[1]
        whole = args[2].shape[3] == BLOCKS * BLOCK
        aligned = half % BLOCK == 0 and args[0].shape[0] % 16 == 0 and rows * CORES == BLOCK
        split = replicas == 8 * CORES and tp_size == 2 and BLOCKS == tp_size * replicas // CORES
        return (grouped if whole and aligned and split else per_device)(*args)

    return jax.shard_map(
        per_part,
        mesh=mesh,
        in_specs=(
            P("dp", "tp"),
            P("dp", "tp"),
            P("dp", "tp", None, None, None),
            P("dp"),
            P("dp", None),
            P(None, ("tp", "dp"), None),
            P(None, ("tp", "dp"), None),
            P(None, ("tp", "dp"), None),
        ),
        out_specs=(
            P("dp", "tp"),
            P(None, ("tp", "dp"), None),
            P(None, ("tp", "dp"), None),
            P(None, ("tp", "dp"), None),
        ),
        check_vma=False,
    )
```

```python
import jax
import jax.numpy as jnp
from jax import lax
from jax.experimental import pallas as pl
from jax.experimental.pallas import tpu as pltpu
from jax.sharding import PartitionSpec as P

BLOCK = 128
BLOCKS = 16


beta_one = 0.9
beta_two = 0.95
learn_rate = 0.05
decay_rate = 0.1
adam_eps = 1e-08
bias_one = 1.0 - 0.9**10
bias_two = 1.0 - 0.95**10


def layout_places(replica_flag, mapping, tp_size, slot_count):
    blocks = jnp.arange(BLOCKS, dtype=jnp.int32)
    canonical = blocks // (BLOCKS // tp_size)
    holder = jnp.where(replica_flag > 0, mapping, canonical)
    earlier = (holder[None, :] == holder[:, None]) & (blocks[None, :] < blocks[:, None])
    slot_rank = jnp.sum(earlier.astype(jnp.int32), axis=1)
    return holder * slot_count + slot_rank


def per_device(tokens, cotangent, working, degraded, block_map, master, moment_one, moment_two):
    tp_size = lax.axis_size("tp")
    replicas = lax.axis_size("dp")
    my_index = lax.axis_index("tp")
    weights = working[0, 0]
    slot_count = weights.shape[1] // BLOCK
    per_dev = BLOCKS // tp_size
    places = layout_places(degraded[0], block_map[0], tp_size, slot_count)
    my_slots = my_index * slot_count + jnp.arange(slot_count, dtype=jnp.int32)
    holding = places[:, None] == my_slots[None, :]
    filled = jnp.any(holding, axis=0).astype(jnp.float32)
    column_mask = jnp.repeat(filled, BLOCK)
    inputs, upstream = (
        lax.all_gather(tokens, "tp", axis=1, tiled=True),
        lax.all_gather(cotangent, "tp", axis=1, tiled=True),
    )
    contract_d = (((1,), (1,)), ((), ()))
    gate_pre = lax.dot_general(inputs, weights[0], contract_d, preferred_element_type=jnp.float32)
    up_pre = lax.dot_general(inputs, weights[1], contract_d, preferred_element_type=jnp.float32)
    hidden_grad = lax.dot_general(
        upstream, weights[2], contract_d, preferred_element_type=jnp.float32
    )
    gate_sig = jax.nn.sigmoid(gate_pre)
    active = gate_pre * gate_sig
    hidden = (active * up_pre * column_mask).astype(jnp.bfloat16)
    gate_grad = (
        hidden_grad * up_pre * gate_sig * (1.0 + gate_pre * (1.0 - gate_sig)) * column_mask
    ).astype(jnp.bfloat16)
    up_grad = (hidden_grad * active * column_mask).astype(jnp.bfloat16)
    partial_value = jnp.dot(gate_grad, weights[0], preferred_element_type=jnp.float32) + jnp.dot(
        up_grad, weights[1], preferred_element_type=jnp.float32
    )
    input_grad = lax.psum_scatter(partial_value, "tp", scatter_dimension=1, tiled=True).astype(
        jnp.bfloat16
    )
    tok_rows = gate_grad.shape[0]
    packed = jnp.stack(
        [
            hidden.reshape(tok_rows, slot_count, BLOCK),
            gate_grad.reshape(tok_rows, slot_count, BLOCK),
            up_grad.reshape(tok_rows, slot_count, BLOCK),
        ],
        axis=2,
    )
    packed = packed.transpose(1, 0, 2, 3).reshape(slot_count, tok_rows, 3 * BLOCK)
    selector = holding.astype(jnp.bfloat16)
    outgoing = jnp.einsum(
        "qs,stc->qtc", selector, packed, preferred_element_type=jnp.float32
    ).astype(jnp.bfloat16)
    incoming = lax.all_to_all(outgoing, "tp", split_axis=0, concat_axis=0, tiled=True)
    owned_acts = jnp.sum(incoming.reshape(tp_size, per_dev, tok_rows, 3 * BLOCK), axis=0)
    owned_kinds = (
        owned_acts.reshape(per_dev, tok_rows, 3, BLOCK)
        .transpose(2, 1, 0, 3)
        .reshape(3, tok_rows, per_dev * BLOCK)
    )
    contract_t = (((0,), (0,)), ((), ()))
    gate_term = lax.dot_general(
        owned_kinds[1], inputs, contract_t, preferred_element_type=jnp.float32
    )
    up_term = lax.dot_general(
        owned_kinds[2], inputs, contract_t, preferred_element_type=jnp.float32
    )
    down_term = lax.dot_general(
        owned_kinds[0], upstream, contract_t, preferred_element_type=jnp.float32
    )
    summed = lax.psum_scatter(
        jnp.stack([gate_term, up_term, down_term], axis=1).astype(jnp.bfloat16),
        "dp",
        scatter_dimension=0,
        tiled=True,
    ).astype(jnp.float32)
    grad_mean = jnp.transpose(summed, (1, 0, 2)) / replicas
    moment_one_next = beta_one * moment_one + (1.0 - beta_one) * grad_mean
    moment_two_next = beta_two * moment_two + (1.0 - beta_two) * grad_mean * grad_mean
    update = (
        moment_one_next / bias_one / (jnp.sqrt(moment_two_next / bias_two) + adam_eps)
        + decay_rate * master
    )
    master_next = master - learn_rate * update
    return (input_grad, master_next, moment_one_next, moment_two_next)


CORES = 2
WIDE = 4 * BLOCK
contract_last = (((1,), (1,)), ((), ()))
contract_mid = (((1,), (0,)), ((), ()))


def dot32(a, b, dims):
    return lax.dot_general(a, b, dims, preferred_element_type=jnp.float32)


FLAG, HOLDER, ME, CORE, NEAR = range(5)


def group_of(i, s, tp_size, depth):
    owner = (s[ME] + 1 + i // depth) % tp_size
    held = jnp.where(s[FLAG] > 0, s[HOLDER] == s[ME], owner == s[ME])
    place = jnp.where(s[FLAG] > 0, owner * depth + i % depth, i % depth)
    return held, jnp.where(held, place, 0)


def weight_specs(kinds, half, sides, layout):
    def spec(kind, side):
        def where(i, s):
            _, place = group_of(i, s, *layout)
            return (0, 0, kind, place, s[ME] if side == 0 else 1 - s[ME])

        return pl.BlockSpec((1, 1, 1, WIDE, half), where)

    return [spec(kind, side) for kind in kinds for side in sides]


def whole_spec(shape):
    return pl.BlockSpec(shape, lambda *_: (0,) * len(shape))


def step_spec(rows):
    return pl.BlockSpec((1, rows, WIDE), lambda i, s: (i, 0, 0))


def own_part(scalars, tokens, cotangent, working, layout):
    steps = layout[0] * layout[1]
    rows, half = tokens.shape

    def body(s, t_ref, c_ref, *refs):
        weights, outs = refs[:3], refs[3:]
        held, _ = group_of(pl.program_id(0), s, *layout)

        @pl.when(held)
        def _():
            for kind, out in enumerate(outs):
                left = c_ref if kind == 2 else t_ref
                out[0] = dot32(left[...], weights[kind][0, 0, 0], contract_last)

    out = jax.ShapeDtypeStruct((steps, rows, WIDE), jnp.float32)
    return pl.pallas_call(
        body,
        out_shape=(out,) * 3,
        grid_spec=pltpu.PrefetchScalarGridSpec(
            num_scalar_prefetch=1,
            grid=(steps,),
            in_specs=[whole_spec(tokens.shape)] * 2 + weight_specs((0, 1, 2), half, (0,), layout),
            out_specs=(step_spec(rows),) * 3,
        ),
        cost_estimate=pl.CostEstimate(
            flops=6 * rows * half * steps * WIDE, bytes_accessed=6 * half * steps * WIDE, transcendentals=0
        ),
        compiler_params=pltpu.CompilerParams(vmem_limit_bytes=34 << 20),
        name="own_part",
    )(scalars, tokens, cotangent, *[working] * 3)


def act_outputs(layout, kinds, rows):
    depth = layout[1]
    block = (2, CORES, 1, kinds, rows, BLOCK)
    shape = jax.ShapeDtypeStruct((2, CORES, depth, kinds, rows, BLOCK), jnp.bfloat16)
    specs = (
        pl.BlockSpec(block, lambda i, s: (0, 0, jnp.minimum(i, depth - 1), 0, 0, 0)),
        pl.BlockSpec(block, lambda i, s: (0, 0, jnp.maximum(i - depth, 0), 0, 0, 0)),
    )
    return (shape, shape), specs


def put_acts(i, s, layout, values, theirs, mine):
    narrow = BLOCK // CORES

    def put(ref):
        for kind, value in enumerate(values):
            for side in range(2):
                for c in range(CORES):
                    starts = [(side * 2 + j) * BLOCK + c * narrow for j in range(2)]
                    piece = jnp.concatenate([value[:, at : at + narrow] for at in starts], axis=1)
                    ref[jnp.bitwise_xor(s[NEAR], side), jnp.bitwise_xor(s[CORE], c), 0, kind] = piece.astype(
                        jnp.bfloat16
                    )

    pl.when(i < layout[1])(lambda: put(theirs))
    pl.when(i >= layout[1])(lambda: put(mine))


def clear_acts(i, layout, theirs, mine):
    def clear(ref):
        ref[...] = jnp.zeros(ref.shape, ref.dtype)

    pl.when(i < layout[1])(lambda: clear(theirs))
    pl.when(i >= layout[1])(lambda: clear(mine))


def gate_up(scalars, other, working, gate, up, layout):
    steps = layout[0] * layout[1]
    rows, half = other.shape

    def body(s, other_ref, w0, w1, gate_ref, up_ref, act_ref, slope_ref, *outs):
        i = pl.program_id(0)
        held, _ = group_of(i, s, *layout)

        @pl.when(held)
        def _():
            zg = gate_ref[0] + dot32(other_ref[...], w0[0, 0, 0], contract_last)
            zu = up_ref[0] + dot32(other_ref[...], w1[0, 0, 0], contract_last)
            sig = jax.nn.sigmoid(zg)
            act = zg * sig
            act_ref[0] = act
            slope_ref[0] = zu * sig * (1.0 + zg * (1.0 - sig))
            put_acts(i, s, layout, [act * zu], *outs)

        pl.when(jnp.logical_not(held))(lambda: clear_acts(i, layout, *outs))

    out = jax.ShapeDtypeStruct((steps, rows, WIDE), jnp.float32)
    shapes, specs = act_outputs(layout, 1, rows)
    return pl.pallas_call(
        body,
        out_shape=(out, out, *shapes),
        grid_spec=pltpu.PrefetchScalarGridSpec(
            num_scalar_prefetch=1,
            grid=(steps,),
            in_specs=[whole_spec(other.shape)] + weight_specs((0, 1), half, (1,), layout) + [step_spec(rows)] * 2,
            out_specs=(step_spec(rows), step_spec(rows), *specs),
        ),
        cost_estimate=pl.CostEstimate(
            flops=4 * rows * half * steps * WIDE,
            bytes_accessed=4 * half * steps * WIDE + 16 * rows * steps * WIDE,
            transcendentals=rows * steps * WIDE,
        ),
        compiler_params=pltpu.CompilerParams(vmem_limit_bytes=28 << 20),
        name="gate_up",
    )(scalars, other, *[working] * 2, gate, up)


def down_acts(scalars, other, working, partial, act, slope, layout):
    steps = layout[0] * layout[1]
    rows, half = other.shape

    def body(s, other_ref, w0, partial_ref, act_ref, slope_ref, grads, *outs):
        i = pl.program_id(0)
        held, _ = group_of(i, s, *layout)

        @pl.when(held)
        def _():
            dh = partial_ref[0] + dot32(other_ref[...], w0[0, 0, 0], contract_last)
            dgate = dh * slope_ref[0]
            dup = dh * act_ref[0]
            grads[0, 0] = dgate.astype(jnp.bfloat16)
            grads[0, 1] = dup.astype(jnp.bfloat16)
            put_acts(i, s, layout, [dgate, dup], *outs)

        pl.when(jnp.logical_not(held))(lambda: clear_acts(i, layout, *outs))

    shapes, specs = act_outputs(layout, 2, rows)
    return pl.pallas_call(
        body,
        out_shape=(jax.ShapeDtypeStruct((steps, 2, rows, WIDE), jnp.bfloat16), *shapes),
        grid_spec=pltpu.PrefetchScalarGridSpec(
            num_scalar_prefetch=1,
            grid=(steps,),
            in_specs=[whole_spec(other.shape)] + weight_specs((2,), half, (1,), layout) + [step_spec(rows)] * 3,
            out_specs=(pl.BlockSpec((1, 2, rows, WIDE), lambda i, s: (i, 0, 0, 0)), *specs),
        ),
        cost_estimate=pl.CostEstimate(
            flops=2 * rows * half * steps * WIDE,
            bytes_accessed=2 * half * steps * WIDE + 20 * rows * steps * WIDE,
            transcendentals=0,
        ),
        compiler_params=pltpu.CompilerParams(vmem_limit_bytes=20 << 20),
        name="down_acts",
    )(scalars, other, working, partial, act, slope)


def input_part(scalars, grads, working, half, side, layout):
    steps = layout[0] * layout[1]
    rows = grads.shape[2]

    def body(s, grads_ref, w0, w1, out_ref, total):
        i = pl.program_id(0)
        held, _ = group_of(i, s, *layout)

        @pl.when(i == 0)
        def _():
            total[...] = jnp.zeros(total.shape, total.dtype)

        @pl.when(held)
        def _():
            total[...] += dot32(grads_ref[0, 0], w0[0, 0, 0], contract_mid) + dot32(
                grads_ref[0, 1], w1[0, 0, 0], contract_mid
            )

        @pl.when(i == steps - 1)
        def _():
            out_ref[...] = total[...].astype(out_ref.dtype)

    return pl.pallas_call(
        body,
        out_shape=jax.ShapeDtypeStruct((rows, half), jnp.bfloat16 if side else jnp.float32),
        grid_spec=pltpu.PrefetchScalarGridSpec(
            num_scalar_prefetch=1,
            grid=(steps,),
            in_specs=[pl.BlockSpec((1, 2, rows, WIDE), lambda i, s: (i, 0, 0, 0))]
            + weight_specs((0, 1), half, (side,), layout),
            out_specs=whole_spec((rows, half)),
            scratch_shapes=[pltpu.VMEM((rows, half), jnp.float32)],
        ),
        cost_estimate=pl.CostEstimate(
            flops=4 * rows * half * steps * WIDE, bytes_accessed=4 * half * steps * WIDE, transcendentals=0
        ),
        compiler_params=pltpu.CompilerParams(vmem_limit_bytes=24 << 20),
        name="input_other" if side else "input_own",
    )(scalars, grads, *[working] * 2)


def weight_grad(acts, inputs, own):
    group = len(acts)
    depth, kinds, rows, _ = acts[0].shape[-4:]
    half = inputs[0].shape[1]
    narrow = BLOCK // CORES
    wide = depth * BLOCK
    owners = wide // narrow
    tile = half // 2 if half % (2 * BLOCK) == 0 else half

    def body(s, *refs):
        a_refs, x_refs, outs = refs[:group], refs[group : 2 * group], refs[2 * group : -2]
        left, value = refs[-2:]

        @pl.when(pl.program_id(0) == 0)
        def _():
            for kind in range(kinds):
                for p in range(depth):
                    column = jnp.concatenate(
                        [ref[0, p, kind] if len(ref.shape) == 5 else ref[p, kind] for ref in a_refs], axis=0
                    )
                    left[kind, p * BLOCK : (p + 1) * BLOCK, :] = column.T

        right = jnp.concatenate([ref[...] for ref in x_refs], axis=0)
        for kind in range(kinds):
            value[...] = dot32(left[kind], right, contract_mid).astype(jnp.bfloat16)
            for relation in range(owners):
                start = pl.multiple_of(jnp.bitwise_xor(s[0], relation) * narrow, narrow)
                piece = value[pl.ds(start, narrow), :]
                if relation == 1:
                    outs[-1][kind * narrow : (kind + 1) * narrow, :] = piece
                else:
                    outs[kind * (owners - 1) + max(relation - 1, 0)][...] = piece

    def act_spec(a):
        if a.ndim == 5:
            return pl.BlockSpec((1, *a.shape[1:]), lambda i, s: (0,) * 5)
        return pl.BlockSpec(a.shape, lambda i, s: (0,) * 4)

    out = jax.ShapeDtypeStruct((narrow, half), jnp.bfloat16)
    made = pl.pallas_call(
        body,
        out_shape=(out,) * (kinds * (owners - 1))
        + (jax.ShapeDtypeStruct((kinds * narrow, half), jnp.bfloat16),),
        grid_spec=pltpu.PrefetchScalarGridSpec(
            num_scalar_prefetch=1,
            grid=(half // tile,),
            in_specs=[act_spec(a) for a in acts] + [pl.BlockSpec((rows, tile), lambda i, s: (0, i))] * group,
            out_specs=(pl.BlockSpec((narrow, tile), lambda i, s: (0, i)),) * (kinds * (owners - 1))
            + (pl.BlockSpec((kinds * narrow, tile), lambda i, s: (0, i)),),
            scratch_shapes=[
                pltpu.VMEM((kinds, wide, group * rows), jnp.bfloat16),
                pltpu.VMEM((wide, tile), jnp.bfloat16),
            ],
        ),
        cost_estimate=pl.CostEstimate(
            flops=2 * kinds * group * rows * wide * half,
            bytes_accessed=2 * group * rows * half + 2 * kinds * wide * half,
            transcendentals=0,
        ),
        compiler_params=pltpu.CompilerParams(vmem_limit_bytes=20 << 20),
    )(own, *acts, *inputs)
    return [made[kind * (owners - 1) : (kind + 1) * (owners - 1)] for kind in range(kinds)], made[-1]


def adam(me, sums, pieces, master, moment_one, moment_two, before, replicas):
    rows, half = sums[0][0][0].shape
    count = len(sums[0])
    steps = len(sums)
    columns = master.shape[2] // half

    def pick(values, i):
        chosen = values[0]
        for at in range(1, steps):
            chosen = jnp.where(i == at, values[at], chosen)
        return chosen

    def at(i, s):
        return (pick([p[0] for p in pieces], i), 0, (s[0] + pick([p[1] for p in pieces], i)) % columns)

    state = pl.BlockSpec((1, rows, half), at)

    def body(s, *refs):
        parts, (master_ref, one_ref, two_ref) = refs[: steps * count], refs[steps * count : steps * count + 3]
        master_out, one_out, two_out = refs[-3:]
        for i in range(steps):

            @pl.when(pl.program_id(0) == i)
            def _(i=i):
                summed = parts[i * count][...].astype(jnp.float32)
                for part in parts[i * count + 1 : (i + 1) * count]:
                    summed = summed + part[...].astype(jnp.float32)
                grad_mean = summed * (1.0 / replicas)
                one = beta_one * one_ref[0] + (1.0 - beta_one) * grad_mean
                two = beta_two * two_ref[0] + (1.0 - beta_two) * grad_mean * grad_mean
                old = master_ref[0]
                update = one * (1.0 / bias_one) / (jnp.sqrt(two * (1.0 / bias_two)) + adam_eps) + decay_rate * old
                master_out[0] = old - learn_rate * update
                one_out[0] = one
                two_out[0] = two

    extra = () if before is None else before
    flat = [part for group in sums for part in group]
    return pl.pallas_call(
        body,
        out_shape=(jax.ShapeDtypeStruct(master.shape, jnp.float32),) * 3,
        grid_spec=pltpu.PrefetchScalarGridSpec(
            num_scalar_prefetch=1,
            grid=(steps,),
            in_specs=[pl.BlockSpec((rows, half), lambda i, s, row=row: (row, 0)) for _, row in flat]
            + [state] * 3
            + [pl.BlockSpec(memory_space=pl.ANY)] * len(extra),
            out_specs=(state,) * 3,
        ),
        input_output_aliases={len(flat) + 4 + i: i for i in range(len(extra))},
        cost_estimate=pl.CostEstimate(
            flops=20 * steps * rows * half, bytes_accessed=28 * steps * rows * half, transcendentals=0
        ),
        compiler_params=pltpu.CompilerParams(vmem_limit_bytes=16 << 20),
        name="adam",
    )(me, *[part for part, _ in flat], master, moment_one, moment_two, *extra)


def grouped(*args):
    return grouped_step(*args)


def grouped_step(tokens, cotangent, working, degraded, block_map, master, moment_one, moment_two):
    replicas = lax.axis_size("dp")
    tp_size = lax.axis_size("tp")
    me = lax.axis_index("tp")
    mine = lax.axis_index("dp")
    core, x = mine % CORES, (mine // CORES) % 2
    zs, zp = (mine // (2 * CORES)) % 2, mine // (4 * CORES)
    per_dev = BLOCKS // tp_size
    half = tokens.shape[1]
    after = lax.optimization_barrier

    def over_y(v):
        return lax.ppermute(v, "tp", [(i, (i + 1) % tp_size) for i in range(tp_size)])

    def over(bit, v):
        pairs = [(i, i ^ bit) for i in range(replicas)]
        return lax.ppermute(v, "dp", pairs)

    def over_core(v):
        return over(1, v)

    def over_x(v):
        return over(CORES, v)

    def over_s(v):
        return over(2 * CORES, v)

    def over_m(v):
        return over(4 * CORES, v)

    layout = (tp_size, per_dev * BLOCK // WIDE)
    scalars = jnp.stack([degraded[0], block_map[0, 0], me, core, zs]).astype(jnp.int32)
    own = (zp * 2 + x).astype(jnp.int32).reshape(1)

    t_own, c_own = tokens, cotangent
    t_other = over_y(t_own)
    c_own_s = over_s(c_own)
    t_own_s = over_s(t_own)
    gate, up, down = own_part(scalars, t_own, c_own, working, layout)
    t_other, c_first = after((t_other, c_own))
    c_other = over_y(c_first)
    c_own_c, t_own_c = over_core(c_own), over_core(t_own)
    act, slope, h_theirs, h_mine = gate_up(scalars, t_other, working, gate, up, layout)
    c_other, h_theirs = after((c_other, h_theirs))
    h_from = over_y(h_theirs)
    c_other_s = over_s(c_other)
    t_other_s = over_s(t_other)
    grads, d_theirs, d_mine = down_acts(scalars, c_other, working, down, act, slope, layout)
    h_from, d_theirs = after((h_from, d_theirs))
    d_from = over_y(d_theirs)

    def spread(mine, came):
        far = mine[1] + came[1]
        near_s = over_s(far)
        near = mine[0] + came[0]
        return [near, near_s, over_core(near[1]), over_core(near_s[1])]

    hidden_acts = spread(h_mine, h_from)
    c_acts = [
        [c_own, c_own_s, c_own_c, over_core(c_own_s)], [c_other, c_other_s, over_core(c_other), over_core(c_other_s)]
    ]
    t_acts = [
        [t_own, t_own_s, t_own_c, over_core(t_own_s)], [t_other, t_other_s, over_core(t_other), over_core(t_other_s)]
    ]
    grad_acts = spread(d_mine, d_from)

    sums = []
    for call in range(4):
        acts, inputs = (hidden_acts, c_acts[call]) if call < 2 else (grad_acts, t_acts[call - 2])
        made, far_x = weight_grad(acts, inputs, own)
        side = over_x(far_x)
        for row, (keep, far_z, far_both) in enumerate(made):
            came = over_x(far_both)
            far_z = (far_z.astype(jnp.float32) + came.astype(jnp.float32)).astype(jnp.bfloat16)
            sums.append(((keep, 0), (side, row), (over_m(far_z), 0)))
    state = None
    for low, high in ((0, 4), (4, 6)):
        state = adam(
            me.astype(jnp.int32).reshape(1),
            sums[low:high],
            PIECES[low:high],
            master,
            moment_one,
            moment_two,
            state,
            replicas,
        )

    sent = over_y(input_part(scalars, grads, working, half, 1, layout))
    kept = input_part(scalars, grads, working, half, 0, layout)
    input_grad = (kept + sent.astype(jnp.float32)).astype(jnp.bfloat16)
    return (input_grad, *state)


PIECES = ((2, 0), (2, 1), (0, 0), (1, 0), (0, 1), (1, 1))


def solution(mesh):
    replicas, tp_size = mesh.shape["dp"], mesh.shape["tp"]

    def per_part(*args):
        half = args[0].shape[1]
        rows = args[5].shape[1]
        whole = args[2].shape[3] == BLOCKS * BLOCK
        aligned = half % BLOCK == 0 and args[0].shape[0] % 16 == 0 and rows * CORES == BLOCK
        split = replicas == 8 * CORES and tp_size == 2 and BLOCKS == tp_size * replicas // CORES
        return (grouped if whole and aligned and split else per_device)(*args)

    return jax.shard_map(
        per_part,
        mesh=mesh,
        in_specs=(
            P("dp", "tp"),
            P("dp", "tp"),
            P("dp", "tp", None, None, None),
            P("dp"),
            P("dp", None),
            P(None, ("tp", "dp"), None),
            P(None, ("tp", "dp"), None),
            P(None, ("tp", "dp"), None),
        ),
        out_specs=(
            P("dp", "tp"),
            P(None, ("tp", "dp"), None),
            P(None, ("tp", "dp"), None),
            P(None, ("tp", "dp"), None),
        ),
        check_vma=False,
    )
```
